32 devices in a mesh: row: 4 (over z), ta: 4 (over y, x), pa: 2 (over core).
Axes of the slice: x: 2, y: 2, z: 4, core: 2. Of those that a mesh axis runs over, the one named last changes fastest.
Arguments:
- density: float32 [16, 256, 512], P('row', 'ta', 'pa'), may hold values from 0.5 to 1.5
- kappa: float32 [16, 256, 512], P('row', 'ta', 'pa'), may hold values from 0.02 to 0.12
Outputs:
- updated: float32 [16, 256, 512], P('row', 'ta', 'pa')
- potential: float32 [16, 256, 512], P('row', 'ta', 'pa')
The draws below stay inside these ranges and needn't reach their ends.
All inputs are finite; a program needn't handle non-finite values.
Results may differ from the reference program's by a relative error of at most 0.0049.
Values sent between devices are 32-bit elements; how exact they have to be, the bound alone decides.
No kernel may reach another device: no remote copies, remote signals or barrier semaphores. Data moves between devices by JAX's collectives and lax.ppermute only.
A program may use at most 64 MiB of HBM per device.

```python
import math
import jax
import jax.numpy as jnp
from jax import lax

DEGREES = 128
NT = 256
NP = 512
NR = 16


def draw_density(key, part):
    base_key = jax.random.fold_in(key, 11)
    noise = jax.random.uniform(base_key, (NR, NT + 2, NP), jnp.float32, -1.0, 1.0)
    lagged = noise - jnp.roll(noise, 2, axis=2)
    pattern = (lagged[:, 2:, :] - lagged[:, :-2, :]) * 0.25
    return (1.0 + 0.5 * pattern).astype(jnp.float32)


def levels(key, extent, shards, low, high):
    factor_of = 1.0
    for position, parts in shards:
        draws = jax.random.uniform(jax.random.fold_in(jax.random.fold_in(key, 6), position), (parts,), jnp.float32, low / len(shards), high / len(shards))
        factor_of = factor_of * jnp.repeat(jnp.exp(draws), extent[position] // parts).reshape((-1,) + (1,) * (len(extent) - 1 - position))
    return factor_of


def setup_inputs(seed: int = 0) -> dict:
    streams_of = jax.random.split(jax.random.key(seed), 3)
    return {
        "density": draw_density(jax.random.fold_in(streams_of[2], 71), 0),
        "kappa": jnp.clip(jnp.exp(math.log(0.12) - 1.7917595 * jax.random.uniform(streams_of[1], (NR, NT, NP), jnp.float32) ** levels(streams_of[1], (NR, NT, NP), ((0, 4), (1, 4), (2, 2)), -0.2, 0.2)), 0.02, 0.12),
    }


HIGH = lax.Precision.HIGHEST

def legendre_table(theta, degrees):
    cos_t = jnp.cos(theta)
    sin_t = jnp.sin(theta)
    order = jnp.arange(degrees).astype(jnp.float32)[:, None]
    first = jnp.where(order == 0.0, 1.0, 0.0) * jnp.ones_like(theta)[None, :]

    def advance(carry, degree):
        prev, older = carry
        lval = degree.astype(jnp.float32)
        below = order < lval
        denom = jnp.where(below, lval * lval - order * order, 1.0)
        coef_a = jnp.sqrt((4.0 * lval * lval - 1.0) / denom)
        lower = lval - 1.0
        numer_b = jnp.maximum(lower * lower - order * order, 0.0)
        coef_b = jnp.sqrt(numer_b / jnp.maximum(4.0 * lower * lower - 1.0, 1.0))
        general = coef_a * (cos_t[None, :] * prev - coef_b * older)
        shifted = jnp.concatenate([jnp.zeros_like(prev[:1]), prev[:-1]], axis=0)
        sect_factor = jnp.where(order == 1.0, jnp.sqrt(3.0), jnp.sqrt((2.0 * order + 1.0) / jnp.maximum(2.0 * order, 1.0)))
        sectoral = sect_factor * sin_t[None, :] * shifted
        fresh = jnp.where(below, general, jnp.where(order == lval, sectoral, 0.0))
        return ((fresh, prev), fresh)
    _, rest = lax.scan(advance, (first, jnp.zeros_like(first)), jnp.arange(1, degrees))
    return jnp.concatenate([first[None], rest], axis=0)

def reference(density, kappa):
    half = NP // 2
    radial_up = jnp.concatenate([density[1:], density[-1:]], 0)
    radial_down = jnp.concatenate([density[:1], density[:-1]], 0)
    north = jnp.roll(density[:, :1], half, axis=2)
    south = jnp.roll(density[:, -1:], half, axis=2)
    polar_up = jnp.concatenate([north, density[:, :-1]], 1)
    polar_down = jnp.concatenate([density[:, 1:], south], 1)
    west = jnp.roll(density, 1, axis=2)
    east = jnp.roll(density, -1, axis=2)
    lap = radial_up + radial_down + polar_up + polar_down + west + east - 6.0 * density
    updated = density + kappa * lap
    log_eight = math.log(8.0)
    shells = jnp.arange(NR).astype(jnp.float32)
    edges_low = jnp.exp(log_eight * (shells / NR - 1.0))
    edges_high = jnp.exp(log_eight * ((shells + 1.0) / NR - 1.0))
    volume = (edges_high ** 3 - edges_low ** 3) / 3.0
    radii = jnp.exp(log_eight * ((shells + 0.5) / NR - 1.0))
    log_step = log_eight / NR
    rows_index = jnp.arange(NT).astype(jnp.float32)
    theta = (rows_index + 0.5) * (math.pi / NT)
    band = jnp.cos(rows_index * (math.pi / NT)) - jnp.cos((rows_index + 1.0) * (math.pi / NT))
    phi = (jnp.arange(NP).astype(jnp.float32) + 0.5) * (2.0 * math.pi / NP)
    modes = jnp.arange(DEGREES).astype(jnp.float32)
    waves = jnp.concatenate([jnp.cos(phi[:, None] * modes[None, :]), jnp.sin(phi[:, None] * modes[None, :])], axis=1)
    weight = updated * volume[:, None, None] * band[None, :, None] * (2.0 * math.pi / NP)
    fourier = jnp.dot(weight.reshape(NR * NT, NP), waves, precision=HIGH).reshape(NR, NT, 2, DEGREES)
    legendre = legendre_table(theta, DEGREES)
    moments = jnp.einsum('rtcm,lmt->rlcm', fourier, legendre, precision=HIGH)
    decay_in = jnp.exp(-log_step * modes)[:, None, None]
    decay_out = jnp.exp(-log_step * (modes + 1.0))[:, None, None]

    def inward(carry, shell):
        fresh = carry * decay_in + shell
        return (fresh, fresh)
    _, inner = lax.scan(inward, jnp.zeros_like(moments[0]), moments)

    def outward(carry, shell):
        beyond, beyond_moment = carry
        fresh = (beyond + beyond_moment) * decay_out
        return ((fresh, shell), fresh)
    zeros = jnp.zeros_like(moments[0])
    _, outer = lax.scan(outward, (zeros, zeros), moments, reverse=True)
    scale = 4.0 * math.pi * (2.0 * modes[None, :] + 1.0) * radii[:, None]
    coeffs = -(inner + outer) / scale[:, :, None, None]
    coeffs = jnp.where(modes[None, :, None, None] > 0.0, coeffs, 0.0)
    spectral = jnp.einsum('rlcm,lmt->rtcm', coeffs, legendre, precision=HIGH)
    potential = jnp.dot(spectral.reshape(NR * NT, 2 * DEGREES), waves.T, precision=HIGH).reshape(NR, NT, NP)
    return (updated, potential)
```

```python
import functools
import math

import jax
import jax.numpy as jnp
import numpy as np
from jax import lax
from jax.experimental import pallas as pl
from jax.experimental.pallas import tpu as pltpu
from jax.sharding import PartitionSpec as P

DEGREES = 128
HIGH = lax.Precision.HIGHEST
AXES = ("row", "ta", "pa")
VMEM = pl.BlockSpec(memory_space=pltpu.VMEM)
SMEM = pl.BlockSpec(memory_space=pltpu.SMEM)


def wave_table(azim_total, parts, owners):
    modes = np.arange(DEGREES).reshape(owners, 1, -1, 1, 1)
    phi = (np.arange(azim_total) + 0.5) * (2.0 * math.pi / azim_total)
    angle = modes * phi.reshape(1, 1, 1, parts, -1)
    both = np.concatenate([np.cos(angle), np.sin(angle)], axis=1)
    rows = 2 * DEGREES
    return both.reshape(rows, parts, -1).transpose(1, 0, 2).astype(np.float32)


def recursion_table(owners):
    l = np.arange(DEGREES, dtype=np.float64)[None, :]
    m = np.arange(DEGREES, dtype=np.float64)[:, None]
    below = m < l
    a = np.sqrt((4 * l * l - 1) / np.where(below, l * l - m * m, 1.0) * below)
    low = l - 1
    b = np.sqrt(np.maximum(low * low - m * m, 0) / np.maximum(4 * low * low - 1, 1.0))
    sect = np.where(l == 1, math.sqrt(3.0), np.sqrt((2 * l + 1) / np.maximum(2 * l, 1.0)))
    first = np.stack([a, a * b]).astype(np.float32)
    per_owner = first.reshape(2, owners, -1).transpose(1, 0, 2)
    return per_owner, sect[0].astype(np.float32)


def legendre_kernel(own, sizes, coef_ref, sect_ref, cos_ref, sin_ref, out_ref):
    owner = own(sizes)
    per, degrees, polar = out_ref.shape
    cos_t = jnp.broadcast_to(cos_ref[...], (8, polar))
    sin_t = jnp.broadcast_to(sin_ref[...], (8, polar))
    sub = lax.broadcasted_iota(jnp.int32, (8, polar), 0)

    def block(step, carry):
        sect, prev, older = carry
        tiles = [jnp.zeros((8, polar), jnp.float32) for _ in range(per)]
        for inner in range(8):
            l = step * 8 + inner
            grown = sect * (sin_t * sect_ref[l])
            sect = jnp.where(l == 0, sect, grown)
            new_prev, new_older = [], []
            for q in range(per):
                a = coef_ref[owner, 0, q * degrees + l]
                b = coef_ref[owner, 1, q * degrees + l]
                fresh = (a * cos_t) * prev[q] - b * older[q]
                fresh = jnp.where(l == owner * per + q, sect, fresh)
                tiles[q] = jnp.where(sub == inner, fresh, tiles[q])
                new_prev.append(fresh)
                new_older.append(prev[q])
            prev, older = new_prev, new_older
        for q in range(per):
            out_ref[q, pl.ds(pl.multiple_of(step * 8, 8), 8), :] = tiles[q]
        return sect, prev, older

    zero = [jnp.zeros((8, polar), jnp.float32) for _ in range(per)]
    lax.fori_loop(0, degrees // 8, block, (jnp.ones((8, polar), jnp.float32), zero, zero))


def stencil_kernel(sizes, rho, kappa, far, below, above, north, south, waves, upd, spec):
    rows, polar, azim = rho.shape
    row, ta, pa = (lax.axis_index(a) for a in AXES)
    lane = lax.broadcasted_iota(jnp.int32, (polar, azim), 1)
    sub = lax.broadcasted_iota(jnp.int32, (polar, azim), 0)
    for r in range(rows):
        c = rho[r]
        p = far[r]
        if r == rows - 1:
            up = jnp.where(row == sizes[0] - 1, c, above[0])
        else:
            up = rho[r + 1]
        if r == 0:
            down = jnp.where(row == 0, c, below[0])
        else:
            down = rho[r - 1]
        first = jnp.where(ta == 0, p[0:1, :], north[r : r + 1, :])
        last = jnp.where(ta == sizes[1] - 1, p[polar - 1 : polar, :], south[r : r + 1, :])
        pol_up = jnp.where(sub == 0, first, pltpu.roll(c, 1, 0))
        pol_down = jnp.where(sub == polar - 1, last, pltpu.roll(c, polar - 1, 0))
        west = pltpu.roll(jnp.where(lane == azim - 1, p, c), 1, 1)
        east = pltpu.roll(jnp.where(lane == 0, p, c), azim - 1, 1)
        lap = up + down + pol_up + pol_down + west + east - 6.0 * c
        upd[r] = c + kappa[r] * lap
    cells = upd[...].reshape(rows * polar, azim)
    spec[...] = lax.dot_general(
        waves[pa], cells, (((1,), (1,)), ((), ())),
        precision=HIGH, preferred_element_type=jnp.float32,
    )


def solve_kernel(own, sizes, rows, polar, spec_ref, leg_ref, band_ref, out_ref, work_ref):
    per, degrees, polar_total = leg_ref.shape
    n_row, n_ta, n_pa = sizes
    shells = rows * n_row
    pair = 2 * per
    owner = own(sizes)
    band = band_ref[...]
    for g in range(n_row):
        parts = []
        for t in range(n_ta):
            base = (g * n_ta + t) * n_pa
            total = spec_ref[base]
            for h in range(1, n_pa):
                total = total + spec_ref[base + h]
            parts.append(total)
        for r in range(rows):
            piece = jnp.concatenate([x[:, r * polar : (r + 1) * polar] for x in parts], axis=1)
            work_ref[g * rows + r] = piece * band
    table = leg_ref[...].reshape(per * degrees, polar_total)
    wide = lax.dot_general(
        work_ref[...].reshape(shells * pair, polar_total), table, (((1,), (1,)), ((), ())),
        precision=HIGH, preferred_element_type=jnp.float32,
    )
    slot = lax.broadcasted_iota(jnp.int32, (shells * pair, degrees), 0) % per
    picked = wide[:, :degrees]
    for q in range(1, per):
        picked = jnp.where(slot == q, wide[:, q * degrees : (q + 1) * degrees], picked)
    log_eight = math.log(8.0)
    step = log_eight / shells
    degree = lax.broadcasted_iota(jnp.int32, (pair, degrees), 1).astype(jnp.float32)
    decay_in = jnp.exp(-step * degree)
    decay_out = jnp.exp(-step * (degree + 1.0))
    scale = jnp.where(degree > 0.0, -1.0 / (4.0 * math.pi * (2.0 * degree + 1.0)), 0.0)
    edges = np.exp(log_eight * (np.arange(shells + 1) / shells - 1.0))
    volume = (edges[1:] ** 3 - edges[:-1] ** 3) / 3.0
    radii = np.exp(log_eight * ((np.arange(shells) + 0.5) / shells - 1.0))
    moments = [picked[i * pair : (i + 1) * pair] * float(volume[i]) for i in range(shells)]
    sums = []
    carry = jnp.zeros((pair, degrees), jnp.float32)
    for i in range(shells):
        carry = carry * decay_in + moments[i]
        sums.append(carry)
    carry = jnp.zeros((pair, degrees), jnp.float32)
    for i in reversed(range(shells)):
        sums[i] = (sums[i] + carry) * (scale * float(1.0 / radii[i]))
        carry = (carry + moments[i]) * decay_out
    coeffs = jnp.concatenate(sums, axis=0)
    spread = jnp.concatenate([jnp.where(slot == q, coeffs, 0.0) for q in range(per)], axis=1)
    field = jnp.dot(spread, table, precision=HIGH, preferred_element_type=jnp.float32)
    for g in range(n_row):
        for t in range(n_ta):
            pieces = [
                field[(g * rows + r) * pair : (g * rows + r + 1) * pair, t * polar : (t + 1) * polar]
                for r in range(rows)
            ]
            block = jnp.concatenate(pieces, axis=1)
            for h in range(n_pa):
                out_ref[(g * n_ta + t) * n_pa + h] = block


def potential_kernel(spec, waves, out):
    rows, polar, azim = out.shape
    pa = lax.axis_index("pa")
    flat = lax.dot_general(
        spec[...], waves[pa], (((0,), (0,)), ((), ())),
        precision=HIGH, preferred_element_type=jnp.float32,
    )
    out[...] = flat.reshape(rows, polar, azim)


def owner_of(sizes):
    row, ta, pa = (lax.axis_index(a) for a in AXES)
    return (row * sizes[1] + ta) * sizes[2] + pa


def shards(sizes, density, kappa):
    rows, polar, azim = density.shape
    n_row, n_ta, n_pa = sizes
    owners = n_row * n_ta * n_pa
    per = DEGREES // owners
    polar_total, azim_total = polar * n_ta, azim * n_pa
    f32 = jnp.float32

    ahead = lambda n: [(i, i + 1) for i in range(n - 1)]
    back = lambda n: [(i + 1, i) for i in range(n - 1)]
    below = lax.ppermute(density[-1:], "row", ahead(n_row))
    above = lax.ppermute(density[:1], "row", back(n_row))
    north = lax.ppermute(density[:, -1, :], "ta", ahead(n_ta))
    south = lax.ppermute(density[:, 0, :], "ta", back(n_ta))
    far = lax.ppermute(density, "pa", [(i, (i + n_pa // 2) % n_pa) for i in range(n_pa)])

    coef, sect = recursion_table(owners)
    edge = np.arange(polar_total + 1) * (math.pi / polar_total)
    theta = (np.arange(polar_total) + 0.5) * (math.pi / polar_total)
    band = (np.cos(edge[:-1]) - np.cos(edge[1:])) * (2.0 * math.pi / azim_total)
    row_of = lambda v: jnp.asarray(v.astype(np.float32)[None, :])
    legendre = pl.pallas_call(
        functools.partial(legendre_kernel, owner_of, sizes),
        out_shape=jax.ShapeDtypeStruct((per, DEGREES, polar_total), f32),
        in_specs=[SMEM, SMEM, VMEM, VMEM],
        out_specs=VMEM,
        cost_estimate=pl.CostEstimate(flops=10**7, bytes_accessed=10**6, transcendentals=0),
        name="legendre",
    )(jnp.asarray(coef), jnp.asarray(sect), row_of(np.cos(theta)), row_of(np.sin(theta)))

    waves = jnp.asarray(wave_table(azim_total, n_pa, owners))
    updated, spec = pl.pallas_call(
        functools.partial(stencil_kernel, sizes),
        out_shape=(
            jax.ShapeDtypeStruct(density.shape, f32),
            jax.ShapeDtypeStruct((2 * DEGREES, rows * polar), f32),
        ),
        in_specs=[VMEM] * 8,
        out_specs=(VMEM, VMEM),
        name="stencil",
    )(density, kappa, far, below, above, north, south, waves)

    spec = lax.all_to_all(
        spec.reshape(owners, 2 * per, rows * polar), AXES, split_axis=0, concat_axis=0, tiled=True
    )
    spec = pl.pallas_call(
        functools.partial(solve_kernel, owner_of, sizes, rows, polar),
        out_shape=jax.ShapeDtypeStruct(spec.shape, f32),
        in_specs=[VMEM] * 3,
        out_specs=VMEM,
        scratch_shapes=[pltpu.VMEM((rows * n_row, 2 * per, polar_total), f32)],
        name="solve",
    )(spec, legendre, row_of(band))
    spec = lax.all_to_all(spec, AXES, split_axis=0, concat_axis=0, tiled=True)

    potential = pl.pallas_call(
        potential_kernel,
        out_shape=jax.ShapeDtypeStruct(density.shape, f32),
        in_specs=[VMEM] * 2,
        out_specs=VMEM,
        name="potential",
    )(spec.reshape(2 * DEGREES, rows * polar), waves)
    return (updated, potential)


def solution(mesh):
    sizes = tuple(mesh.shape[a] for a in AXES)
    placed = (P(*AXES), P(*AXES))
    return jax.shard_map(
        functools.partial(shards, sizes), mesh=mesh, in_specs=placed, out_specs=placed, check_vma=False
    )
```

```python
import functools
import math

import jax
import jax.numpy as jnp
import numpy as np
from jax import lax
from jax.experimental import pallas as pl
from jax.experimental.pallas import tpu as pltpu
from jax.sharding import PartitionSpec as P

DEGREES = 128
HIGH = lax.Precision.HIGHEST
AXES = ("row", "ta", "pa")
VMEM = pl.BlockSpec(memory_space=pltpu.VMEM)
SMEM = pl.BlockSpec(memory_space=pltpu.SMEM)
PARAMS = pltpu.CompilerParams(vmem_limit_bytes=16 * 2**20)


def wave_table(azim_total, owners):
    modes = np.arange(DEGREES).reshape(owners, 1, -1, 1)
    phi = (np.arange(azim_total) + 0.5) * (2.0 * math.pi / azim_total)
    both = np.concatenate([np.cos(modes * phi), np.sin(modes * phi)], axis=1)
    return both.reshape(2 * DEGREES, azim_total).astype(np.float32)


def recursion_table(owners):
    l = np.arange(DEGREES, dtype=np.float64)[None, :]
    m = np.arange(DEGREES, dtype=np.float64)[:, None]
    below = m < l
    a = np.sqrt((4 * l * l - 1) / np.where(below, l * l - m * m, 1.0) * below)
    low = l - 1
    b = np.sqrt(np.maximum(low * low - m * m, 0) / np.maximum(4 * low * low - 1, 1.0))
    sect = np.where(l == 1, math.sqrt(3.0), np.sqrt((2 * l + 1) / np.maximum(2 * l, 1.0)))
    first = np.stack([a, a * b]).astype(np.float32)
    per_owner = first.reshape(2, owners, -1).transpose(1, 0, 2)
    return per_owner, sect[0].astype(np.float32)


def legendre_kernel(own, sizes, coef_ref, sect_ref, cos_ref, sin_ref, out_ref):
    owner = own(sizes)
    per, degrees, polar = out_ref.shape
    cos_t = jnp.broadcast_to(cos_ref[...], (8, polar))
    sin_t = jnp.broadcast_to(sin_ref[...], (8, polar))
    sub = lax.broadcasted_iota(jnp.int32, (8, polar), 0)

    def block(step, carry):
        sect, prev, older = carry
        tiles = [jnp.zeros((8, polar), jnp.float32) for _ in range(per)]
        for inner in range(8):
            l = step * 8 + inner
            grown = sect * (sin_t * sect_ref[l])
            sect = jnp.where(l == 0, sect, grown)
            new_prev, new_older = [], []
            for q in range(per):
                a = coef_ref[owner, 0, q * degrees + l]
                b = coef_ref[owner, 1, q * degrees + l]
                fresh = (a * cos_t) * prev[q] - b * older[q]
                fresh = jnp.where(l == owner * per + q, sect, fresh)
                tiles[q] = jnp.where(sub == inner, fresh, tiles[q])
                new_prev.append(fresh)
                new_older.append(prev[q])
            prev, older = new_prev, new_older
        for q in range(per):
            out_ref[q, pl.ds(pl.multiple_of(step * 8, 8), 8), :] = tiles[q]
        return sect, prev, older

    zero = [jnp.zeros((8, polar), jnp.float32) for _ in range(per)]
    lax.fori_loop(0, degrees // 8, block, (jnp.ones((8, polar), jnp.float32), zero, zero))


def pair_swap(value, axes, count, first):
    pairs = []
    for i in range(first, count - 1, 2):
        pairs += [(i, i + 1), (i + 1, i)]
    return lax.ppermute(value, axes, pairs)


def joined(pa, own, far):
    return jnp.concatenate([jnp.where(pa == 0, own, far), jnp.where(pa == 0, far, own)], axis=1)


def pack_kernel(rho, far, shell_out, even_out, odd_out):
    rows, polar, azim = rho.shape
    half = rows // 2
    ta, pa = lax.axis_index("ta"), lax.axis_index("pa")
    edge = pa * (rows - 1)
    shell_out[...] = joined(pa, rho[edge], far[edge])
    even = ta % 2 == 0
    for r in range(half):
        own, other = rho.at[pa * half + r], far.at[pa * half + r]
        top = joined(pa, own[0:1, :], other[0:1, :])
        low = joined(pa, own[polar - 1 : polar, :], other[polar - 1 : polar, :])
        even_out[r : r + 1, :] = jnp.where(even, low, top)
        odd_out[r : r + 1, :] = jnp.where(even, top, low)


def stencil_kernel(sizes, rho, far, kappa, far_kappa, shell, even_in, odd_in, waves, keep, send, spec, cells):
    rows, polar, azim = rho.shape
    half = rows // 2
    row, ta, pa = (lax.axis_index(a) for a in AXES)
    even = ta % 2 == 0
    sub = lax.broadcasted_iota(jnp.int32, (polar, 2 * azim), 0)
    at = lambda i: joined(pa, rho[i], far[i])
    for r in range(half):
        i = pa * half + r
        c = at(i)
        if r == 0:
            ghost = jnp.where(row == 0, c, shell[...])
            down = jnp.where(pa == 0, ghost, at(jnp.maximum(i - 1, 0)))
        else:
            down = at(i - 1)
        if r == half - 1:
            ghost = jnp.where(row == sizes[0] - 1, c, shell[...])
            up = jnp.where(pa == 0, at(jnp.minimum(i + 1, rows - 1)), ghost)
        else:
            up = at(i + 1)
        north = jnp.where(even, odd_in[r : r + 1, :], even_in[r : r + 1, :])
        south = jnp.where(even, even_in[r : r + 1, :], odd_in[r : r + 1, :])
        north = jnp.where(ta == 0, pltpu.roll(c[0:1, :], azim, 1), north)
        south = jnp.where(ta == sizes[1] - 1, pltpu.roll(c[polar - 1 :, :], azim, 1), south)
        pol_up = jnp.where(sub == 0, north, pltpu.roll(c, 1, 0))
        pol_down = jnp.where(sub == polar - 1, south, pltpu.roll(c, polar - 1, 0))
        west = pltpu.roll(c, 1, 1)
        east = pltpu.roll(c, 2 * azim - 1, 1)
        lap = up + down + pol_up + pol_down + west + east - 6.0 * c
        new = c + joined(pa, kappa[i], far_kappa[i]) * lap
        keep[r] = jnp.where(pa == 0, new[:, :azim], new[:, azim:])
        send[r] = jnp.where(pa == 0, new[:, azim:], new[:, :azim])
        cells[r * polar : (r + 1) * polar, :] = new
    spec[...] = lax.dot_general(
        waves[...], cells[...], (((1,), (1,)), ((), ())),
        precision=HIGH, preferred_element_type=jnp.float32,
    )


def solve_kernel(own, sizes, rows, polar, spec_ref, leg_ref, band_ref, out_ref, work_ref):
    per, degrees, polar_total = leg_ref.shape
    n_row, n_ta, n_pa = sizes
    shells = rows * n_row
    pair = 2 * per
    owner = own(sizes)
    band = band_ref[...]
    half = rows // n_pa
    for g in range(n_row):
        for h in range(n_pa):
            parts = [spec_ref[(g * n_ta + t) * n_pa + h] for t in range(n_ta)]
            for r in range(half):
                piece = jnp.concatenate([x[:, r * polar : (r + 1) * polar] for x in parts], axis=1)
                work_ref[g * rows + h * half + r] = piece * band
    table = leg_ref[...].reshape(per * degrees, polar_total)
    wide = lax.dot_general(
        work_ref[...].reshape(shells * pair, polar_total), table, (((1,), (1,)), ((), ())),
        precision=HIGH, preferred_element_type=jnp.float32,
    )
    slot = lax.broadcasted_iota(jnp.int32, (shells * pair, degrees), 0) % per
    picked = wide[:, :degrees]
    for q in range(1, per):
        picked = jnp.where(slot == q, wide[:, q * degrees : (q + 1) * degrees], picked)
    log_eight = math.log(8.0)
    step = log_eight / shells
    degree = lax.broadcasted_iota(jnp.int32, (pair, degrees), 1).astype(jnp.float32)
    decay_in = jnp.exp(-step * degree)
    decay_out = jnp.exp(-step * (degree + 1.0))
    scale = jnp.where(degree > 0.0, -1.0 / (4.0 * math.pi * (2.0 * degree + 1.0)), 0.0)
    edges = np.exp(log_eight * (np.arange(shells + 1) / shells - 1.0))
    volume = (edges[1:] ** 3 - edges[:-1] ** 3) / 3.0
    radii = np.exp(log_eight * ((np.arange(shells) + 0.5) / shells - 1.0))
    moments = [picked[i * pair : (i + 1) * pair] * float(volume[i]) for i in range(shells)]
    sums = []
    carry = jnp.zeros((pair, degrees), jnp.float32)
    for i in range(shells):
        carry = carry * decay_in + moments[i]
        sums.append(carry)
    carry = jnp.zeros((pair, degrees), jnp.float32)
    for i in reversed(range(shells)):
        sums[i] = (sums[i] + carry) * (scale * float(1.0 / radii[i]))
        carry = (carry + moments[i]) * decay_out
    coeffs = jnp.concatenate(sums, axis=0)
    spread = jnp.concatenate([jnp.where(slot == q, coeffs, 0.0) for q in range(per)], axis=1)
    field = jnp.dot(spread, table, precision=HIGH, preferred_element_type=jnp.float32)
    for g in range(n_row):
        for h in range(n_pa):
            for t in range(n_ta):
                pieces = []
                for r in range(half):
                    i = g * rows + h * half + r
                    pieces.append(field[i * pair : (i + 1) * pair, t * polar : (t + 1) * polar])
                out_ref[(g * n_ta + t) * n_pa + h] = jnp.concatenate(pieces, axis=1)


def potential_kernel(spec, far, waves, out):
    rows, polar, azim = out.shape
    half = rows // 2
    pa = lax.axis_index("pa")
    table = waves[:, pl.ds(pl.multiple_of(pa * azim, azim), azim)]
    for part, place in ((spec, pa), (far, 1 - pa)):
        flat = lax.dot_general(
            part[...], table, (((0,), (0,)), ((), ())),
            precision=HIGH, preferred_element_type=jnp.float32,
        )
        out[pl.ds(place * half, half)] = flat.reshape(half, polar, azim)


def owner_of(sizes):
    row, ta, pa = (lax.axis_index(a) for a in AXES)
    return (row * sizes[1] + ta) * sizes[2] + pa


def shards(sizes, density, kappa):
    rows, polar, azim = density.shape
    n_row, n_ta, n_pa = sizes
    owners = n_row * n_ta * n_pa
    per = DEGREES // owners
    polar_total, azim_total = polar * n_ta, azim * n_pa
    f32 = jnp.float32

    half = rows // n_pa
    swap = functools.partial(pair_swap, axes="pa", count=n_pa, first=0)
    far, far_kappa = swap(density), swap(kappa)
    edges = pl.pallas_call(
        pack_kernel,
        out_shape=(
            jax.ShapeDtypeStruct((polar, azim_total), f32),
            jax.ShapeDtypeStruct((half, azim_total), f32),
            jax.ShapeDtypeStruct((half, azim_total), f32),
        ),
        in_specs=[VMEM] * 2,
        out_specs=(VMEM,) * 3,
        compiler_params=PARAMS,
        name="pack",
    )(density, far)
    shell = pair_swap(edges[0], ("row", "pa"), n_row * n_pa, 1)
    even_in = pair_swap(edges[1], "ta", n_ta, 0)
    odd_in = pair_swap(edges[2], "ta", n_ta, 1)

    coef, sect = recursion_table(owners)
    edge = np.arange(polar_total + 1) * (math.pi / polar_total)
    theta = (np.arange(polar_total) + 0.5) * (math.pi / polar_total)
    band = (np.cos(edge[:-1]) - np.cos(edge[1:])) * (2.0 * math.pi / azim_total)
    row_of = lambda v: jnp.asarray(v.astype(np.float32)[None, :])
    legendre = pl.pallas_call(
        functools.partial(legendre_kernel, owner_of, sizes),
        out_shape=jax.ShapeDtypeStruct((per, DEGREES, polar_total), f32),
        in_specs=[SMEM, SMEM, VMEM, VMEM],
        out_specs=VMEM,
        cost_estimate=pl.CostEstimate(flops=10**7, bytes_accessed=10**6, transcendentals=0),
        compiler_params=PARAMS,
        name="legendre",
    )(jnp.asarray(coef), jnp.asarray(sect), row_of(np.cos(theta)), row_of(np.sin(theta)))

    waves = jnp.asarray(wave_table(azim_total, owners))
    cells = half * polar
    keep, send, spec = pl.pallas_call(
        functools.partial(stencil_kernel, sizes),
        out_shape=(
            jax.ShapeDtypeStruct((half, polar, azim), f32),
            jax.ShapeDtypeStruct((half, polar, azim), f32),
            jax.ShapeDtypeStruct((2 * DEGREES, cells), f32),
        ),
        in_specs=[VMEM] * 8,
        out_specs=(VMEM,) * 3,
        scratch_shapes=[pltpu.VMEM((cells, azim_total), f32)],
        compiler_params=PARAMS,
        name="stencil",
    )(density, far, kappa, far_kappa, shell, even_in, odd_in, waves)

    spread = functools.partial(
        lax.all_to_all, axis_name=AXES, split_axis=0, concat_axis=0, tiled=True
    )
    spec = spread(spec.reshape(owners, 2 * per, cells))
    back = swap(send)
    first = lax.axis_index("pa") == 0
    updated = jnp.concatenate([jnp.where(first, keep, back), jnp.where(first, back, keep)])
    spec = pl.pallas_call(
        functools.partial(solve_kernel, owner_of, sizes, rows, polar),
        out_shape=jax.ShapeDtypeStruct(spec.shape, f32),
        in_specs=[VMEM] * 3,
        out_specs=VMEM,
        scratch_shapes=[pltpu.VMEM((rows * n_row, 2 * per, polar_total), f32)],
        compiler_params=PARAMS,
        name="solve",
    )(spec, legendre, row_of(band))
    spec = spread(spec).reshape(2 * DEGREES, cells)
    potential = pl.pallas_call(
        potential_kernel,
        out_shape=jax.ShapeDtypeStruct(density.shape, f32),
        in_specs=[VMEM] * 3,
        out_specs=VMEM,
        compiler_params=PARAMS,
        name="potential",
    )(spec, swap(spec), waves)
    return (updated, potential)


def solution(mesh):
    sizes = tuple(mesh.shape[a] for a in AXES)
    placed = (P(*AXES), P(*AXES))
    return jax.shard_map(
        functools.partial(shards, sizes), mesh=mesh, in_specs=placed, out_specs=placed, check_vma=False
    )
```

```python
import functools
import math

import jax
import jax.numpy as jnp
import numpy as np
from jax import lax
from jax.experimental import pallas as pl
from jax.experimental.pallas import tpu as pltpu
from jax.sharding import PartitionSpec as P

DEGREES = 128
HIGH = lax.Precision.HIGHEST
AXES = ("row", "ta", "pa")
VMEM = pl.BlockSpec(memory_space=pltpu.VMEM)
SMEM = pl.BlockSpec(memory_space=pltpu.SMEM)
PARAMS = pltpu.CompilerParams(vmem_limit_bytes=16 * 2**20)


def wave_table(azim_total, owners):
    modes = np.arange(DEGREES).reshape(owners, 1, -1, 1)
    phi = (np.arange(azim_total) + 0.5) * (2.0 * math.pi / azim_total)
    both = np.concatenate([np.cos(modes * phi), np.sin(modes * phi)], axis=1)
    return both.reshape(2 * DEGREES, azim_total).astype(np.float32)


def recursion_table(owners):
    l = np.arange(DEGREES, dtype=np.float64)[None, :]
    m = np.arange(DEGREES, dtype=np.float64)[:, None]
    below = m < l
    a = np.sqrt((4 * l * l - 1) / np.where(below, l * l - m * m, 1.0) * below)
    low = l - 1
    b = np.sqrt(np.maximum(low * low - m * m, 0) / np.maximum(4 * low * low - 1, 1.0))
    sect = np.where(l == 1, math.sqrt(3.0), np.sqrt((2 * l + 1) / np.maximum(2 * l, 1.0)))
    first = np.stack([a, a * b]).astype(np.float32)
    per_owner = first.reshape(2, owners, -1).transpose(1, 0, 2)
    return per_owner, sect[0].astype(np.float32)


def legendre_kernel(own, sizes, coef_ref, sect_ref, cos_ref, sin_ref, out_ref):
    owner = own(sizes)
    per, degrees, polar = out_ref.shape
    cos_t = jnp.broadcast_to(cos_ref[...], (8, polar))
    sin_t = jnp.broadcast_to(sin_ref[...], (8, polar))
    sub = lax.broadcasted_iota(jnp.int32, (8, polar), 0)

    def block(step, carry):
        sect, prev, older = carry
        tiles = [jnp.zeros((8, polar), jnp.float32) for _ in range(per)]
        for inner in range(8):
            l = step * 8 + inner
            grown = sect * (sin_t * sect_ref[l])
            sect = jnp.where(l == 0, sect, grown)
            new_prev, new_older = [], []
            for q in range(per):
                a = coef_ref[owner, 0, q * degrees + l]
                b = coef_ref[owner, 1, q * degrees + l]
                fresh = (a * cos_t) * prev[q] - b * older[q]
                fresh = jnp.where(l == owner * per + q, sect, fresh)
                tiles[q] = jnp.where(sub == inner, fresh, tiles[q])
                new_prev.append(fresh)
                new_older.append(prev[q])
            prev, older = new_prev, new_older
        for q in range(per):
            out_ref[q, pl.ds(pl.multiple_of(step * 8, 8), 8), :] = tiles[q]
        return sect, prev, older

    zero = [jnp.zeros((8, polar), jnp.float32) for _ in range(per)]
    lax.fori_loop(0, degrees // 8, block, (jnp.ones((8, polar), jnp.float32), zero, zero))


def pair_swap(value, axes, count, first):
    pairs = []
    for i in range(first, count - 1, 2):
        pairs += [(i, i + 1), (i + 1, i)]
    return lax.ppermute(value, axes, pairs)


def polar_pairs(n_ta, n_pa):
    pairs = []
    for core in range(2):
        for t in range(core, n_ta - 1, 2):
            here, there = t * n_pa + core, (t + 1) * n_pa + core
            pairs += [(here, there), (there, here)]
    return pairs


def joined(pa, own, far):
    return jnp.concatenate([jnp.where(pa == 0, own, far), jnp.where(pa == 0, far, own)], axis=1)


def stage_kernel(rho, kappa, rho_out, kappa_out):
    rho_out[...] = rho[...]
    kappa_out[...] = kappa[...]


def pack_kernel(rho, far, shell_out, ends_out):
    rows, polar, azim = rho.shape
    ta, pa = lax.axis_index("ta"), lax.axis_index("pa")
    edge = pa * (rows - 1)
    shell_out[...] = joined(pa, rho[edge], far[edge])
    low = ta % 2 == pa
    for r in range(rows):
        first = joined(pa, rho[r, 0:1, :], far[r, 0:1, :])
        last = joined(pa, rho[r, polar - 1 : polar, :], far[r, polar - 1 : polar, :])
        ends_out[r : r + 1, :] = jnp.where(low, last, first)


def stencil_kernel(sizes, rho, far, kappa, far_kappa, shell, mine, theirs, waves, keep, send, spec, cells):
    rows, polar, azim = rho.shape
    half = rows // 2
    row, ta, pa = (lax.axis_index(a) for a in AXES)
    low = ta % 2 == pa
    sub = lax.broadcasted_iota(jnp.int32, (polar, 2 * azim), 0)
    at = lambda i: joined(pa, rho[i], far[i])
    for r in range(half):
        i = pa * half + r
        c = at(i)
        if r == 0:
            ghost = jnp.where(row == 0, c, shell[...])
            down = jnp.where(pa == 0, ghost, at(jnp.maximum(i - 1, 0)))
        else:
            down = at(i - 1)
        if r == half - 1:
            ghost = jnp.where(row == sizes[0] - 1, c, shell[...])
            up = jnp.where(pa == 0, at(jnp.minimum(i + 1, rows - 1)), ghost)
        else:
            up = at(i + 1)
        north = jnp.where(low, theirs[pl.ds(i, 1), :], mine[pl.ds(i, 1), :])
        south = jnp.where(low, mine[pl.ds(i, 1), :], theirs[pl.ds(i, 1), :])
        north = jnp.where(ta == 0, pltpu.roll(c[0:1, :], azim, 1), north)
        south = jnp.where(ta == sizes[1] - 1, pltpu.roll(c[polar - 1 :, :], azim, 1), south)
        pol_up = jnp.where(sub == 0, north, pltpu.roll(c, 1, 0))
        pol_down = jnp.where(sub == polar - 1, south, pltpu.roll(c, polar - 1, 0))
        west = pltpu.roll(c, 1, 1)
        east = pltpu.roll(c, 2 * azim - 1, 1)
        lap = up + down + pol_up + pol_down + west + east - 6.0 * c
        new = c + joined(pa, kappa[i], far_kappa[i]) * lap
        keep[r] = jnp.where(pa == 0, new[:, :azim], new[:, azim:])
        send[r] = jnp.where(pa == 0, new[:, azim:], new[:, :azim])
        cells[r * polar : (r + 1) * polar, :] = new
    spec[...] = lax.dot_general(
        waves[...], cells[...], (((1,), (1,)), ((), ())),
        precision=HIGH, preferred_element_type=jnp.float32,
    )


def solve_kernel(own, sizes, rows, polar, spec_ref, leg_ref, band_ref, out_ref, work_ref):
    per, degrees, polar_total = leg_ref.shape
    n_row, n_ta, n_pa = sizes
    shells = rows * n_row
    pair = 2 * per
    owner = own(sizes)
    band = band_ref[...]
    half = rows // n_pa
    for g in range(n_row):
        for h in range(n_pa):
            parts = [spec_ref[(g * n_ta + t) * n_pa + h] for t in range(n_ta)]
            for r in range(half):
                piece = jnp.concatenate([x[:, r * polar : (r + 1) * polar] for x in parts], axis=1)
                work_ref[g * rows + h * half + r] = piece * band
    table = leg_ref[...].reshape(per * degrees, polar_total)
    wide = lax.dot_general(
        work_ref[...].reshape(shells * pair, polar_total), table, (((1,), (1,)), ((), ())),
        precision=HIGH, preferred_element_type=jnp.float32,
    )
    slot = lax.broadcasted_iota(jnp.int32, (shells * pair, degrees), 0) % per
    picked = wide[:, :degrees]
    for q in range(1, per):
        picked = jnp.where(slot == q, wide[:, q * degrees : (q + 1) * degrees], picked)
    log_eight = math.log(8.0)
    step = log_eight / shells
    degree = lax.broadcasted_iota(jnp.int32, (pair, degrees), 1).astype(jnp.float32)
    decay_in = jnp.exp(-step * degree)
    decay_out = jnp.exp(-step * (degree + 1.0))
    scale = jnp.where(degree > 0.0, -1.0 / (4.0 * math.pi * (2.0 * degree + 1.0)), 0.0)
    edges = np.exp(log_eight * (np.arange(shells + 1) / shells - 1.0))
    volume = (edges[1:] ** 3 - edges[:-1] ** 3) / 3.0
    radii = np.exp(log_eight * ((np.arange(shells) + 0.5) / shells - 1.0))
    moments = [picked[i * pair : (i + 1) * pair] * float(volume[i]) for i in range(shells)]
    sums = []
    carry = jnp.zeros((pair, degrees), jnp.float32)
    for i in range(shells):
        carry = carry * decay_in + moments[i]
        sums.append(carry)
    carry = jnp.zeros((pair, degrees), jnp.float32)
    for i in reversed(range(shells)):
        sums[i] = (sums[i] + carry) * (scale * float(1.0 / radii[i]))
        carry = (carry + moments[i]) * decay_out
    coeffs = jnp.concatenate(sums, axis=0)
    spread = jnp.concatenate([jnp.where(slot == q, coeffs, 0.0) for q in range(per)], axis=1)
    field = jnp.dot(spread, table, precision=HIGH, preferred_element_type=jnp.float32)
    for g in range(n_row):
        for h in range(n_pa):
            for t in range(n_ta):
                pieces = []
                for r in range(half):
                    i = g * rows + h * half + r
                    pieces.append(field[i * pair : (i + 1) * pair, t * polar : (t + 1) * polar])
                out_ref[(g * n_ta + t) * n_pa + h] = jnp.concatenate(pieces, axis=1)


def potential_kernel(spec, far, waves, out):
    rows, polar, azim = out.shape
    half = rows // 2
    pa = lax.axis_index("pa")
    table = waves[:, pl.ds(pl.multiple_of(pa * azim, azim), azim)]
    for part, place in ((spec, pa), (far, 1 - pa)):
        flat = lax.dot_general(
            part[...], table, (((0,), (0,)), ((), ())),
            precision=HIGH, preferred_element_type=jnp.float32,
        )
        out[pl.ds(place * half, half)] = flat.reshape(half, polar, azim)


def owner_of(sizes):
    row, ta, pa = (lax.axis_index(a) for a in AXES)
    return (row * sizes[1] + ta) * sizes[2] + pa


def shards(sizes, density, kappa):
    rows, polar, azim = density.shape
    n_row, n_ta, n_pa = sizes
    owners = n_row * n_ta * n_pa
    per = DEGREES // owners
    polar_total, azim_total = polar * n_ta, azim * n_pa
    f32 = jnp.float32

    half = rows // n_pa
    swap = functools.partial(pair_swap, axes="pa", count=n_pa, first=0)
    far, far_kappa = swap(density), swap(kappa)
    density, kappa = pl.pallas_call(
        stage_kernel,
        out_shape=(jax.ShapeDtypeStruct(density.shape, f32),) * 2,
        in_specs=[VMEM] * 2,
        out_specs=(VMEM,) * 2,
        compiler_params=PARAMS,
        cost_estimate=pl.CostEstimate(flops=0, bytes_accessed=2**20, transcendentals=0),
        name="stage",
    )(density, kappa)
    shell, ends = pl.pallas_call(
        pack_kernel,
        out_shape=(
            jax.ShapeDtypeStruct((polar, azim_total), f32),
            jax.ShapeDtypeStruct((rows, azim_total), f32),
        ),
        in_specs=[VMEM] * 2,
        out_specs=(VMEM,) * 2,
        compiler_params=PARAMS,
        name="pack",
    )(density, far)
    mine = lax.ppermute(ends, ("ta", "pa"), polar_pairs(n_ta, n_pa))
    shell = pair_swap(shell, ("row", "pa"), n_row * n_pa, 1)
    theirs = swap(mine)

    coef, sect = recursion_table(owners)
    edge = np.arange(polar_total + 1) * (math.pi / polar_total)
    theta = (np.arange(polar_total) + 0.5) * (math.pi / polar_total)
    band = (np.cos(edge[:-1]) - np.cos(edge[1:])) * (2.0 * math.pi / azim_total)
    row_of = lambda v: jnp.asarray(v.astype(np.float32)[None, :])
    legendre = pl.pallas_call(
        functools.partial(legendre_kernel, owner_of, sizes),
        out_shape=jax.ShapeDtypeStruct((per, DEGREES, polar_total), f32),
        in_specs=[SMEM, SMEM, VMEM, VMEM],
        out_specs=VMEM,
        cost_estimate=pl.CostEstimate(flops=10**7, bytes_accessed=10**6, transcendentals=0),
        compiler_params=PARAMS,
        name="legendre",
    )(jnp.asarray(coef), jnp.asarray(sect), row_of(np.cos(theta)), row_of(np.sin(theta)))

    waves = jnp.asarray(wave_table(azim_total, owners))
    cells = half * polar
    keep, send, spec = pl.pallas_call(
        functools.partial(stencil_kernel, sizes),
        out_shape=(
            jax.ShapeDtypeStruct((half, polar, azim), f32),
            jax.ShapeDtypeStruct((half, polar, azim), f32),
            jax.ShapeDtypeStruct((2 * DEGREES, cells), f32),
        ),
        in_specs=[VMEM] * 8,
        out_specs=(VMEM,) * 3,
        scratch_shapes=[pltpu.VMEM((cells, azim_total), f32)],
        compiler_params=PARAMS,
        name="stencil",
    )(density, far, kappa, far_kappa, shell, mine, theirs, waves)

    spread = functools.partial(
        lax.all_to_all, axis_name=AXES, split_axis=0, concat_axis=0, tiled=True
    )
    spec = spread(spec.reshape(owners, 2 * per, cells))
    back = swap(send)
    first = lax.axis_index("pa") == 0
    updated = jnp.concatenate([jnp.where(first, keep, back), jnp.where(first, back, keep)])
    spec = pl.pallas_call(
        functools.partial(solve_kernel, owner_of, sizes, rows, polar),
        out_shape=jax.ShapeDtypeStruct(spec.shape, f32),
        in_specs=[VMEM] * 3,
        out_specs=VMEM,
        scratch_shapes=[pltpu.VMEM((rows * n_row, 2 * per, polar_total), f32)],
        compiler_params=PARAMS,
        name="solve",
    )(spec, legendre, row_of(band))
    spec = spread(spec).reshape(2 * DEGREES, cells)
    potential = pl.pallas_call(
        potential_kernel,
        out_shape=jax.ShapeDtypeStruct(density.shape, f32),
        in_specs=[VMEM] * 3,
        out_specs=VMEM,
        compiler_params=PARAMS,
        name="potential",
    )(spec, swap(spec), waves)
    return (updated, potential)


def solution(mesh):
    sizes = tuple(mesh.shape[a] for a in AXES)
    placed = (P(*AXES), P(*AXES))
    return jax.shard_map(
        functools.partial(shards, sizes), mesh=mesh, in_specs=placed, out_specs=placed, check_vma=False
    )
```

```python
import functools
import math

import jax
import jax.numpy as jnp
import numpy as np
from jax import lax
from jax.experimental import pallas as pl
from jax.experimental.pallas import tpu as pltpu
from jax.sharding import PartitionSpec as P


DEGREES = 128
AXES = ("row", "ta", "pa")
VMEM = pl.BlockSpec(memory_space=pltpu.VMEM)
PARAMS = pltpu.CompilerParams(vmem_limit_bytes=16 * 2**20)
F32 = jnp.float32
BF16 = jnp.bfloat16
NT = (((1,), (1,)), ((), ()))
NN = (((1,), (0,)), ((), ()))
TN = (((0,), (0,)), ((), ()))


def split(x):
    high = x.astype(BF16)
    return high, (x - high.astype(F32)).astype(BF16)


def dot3(a, b, dims):
    one = functools.partial(lax.dot_general, dimension_numbers=dims, preferred_element_type=F32)
    return one(a[0], b[0]) + (one(a[0], b[1]) + one(a[1], b[0]))


def wave_table(azim_total, owners):
    modes = np.arange(DEGREES).reshape(owners, 1, -1, 1)
    phi = (np.arange(azim_total) + 0.5) * (2.0 * math.pi / azim_total)
    both = np.concatenate([np.cos(modes * phi), np.sin(modes * phi)], axis=1)
    table = both.reshape(2 * DEGREES, azim_total)
    high = table.astype(BF16)
    low = (table - high.astype(np.float64)).astype(BF16)
    return jnp.asarray(high), jnp.asarray(low)


def recursion_table():
    l = np.arange(DEGREES, dtype=np.float64)[:, None]
    m = np.arange(DEGREES, dtype=np.float64)[None, :]
    below = m < l
    a = np.sqrt((4 * l * l - 1) / np.where(below, l * l - m * m, 1.0) * below)
    low = l - 1
    b = np.sqrt(np.maximum(low * low - m * m, 0) / np.maximum(4 * low * low - 1, 1.0))
    sect = np.where(l == 1, math.sqrt(3.0), np.sqrt((2 * l + 1) / np.maximum(2 * l, 1.0)))
    wide = np.broadcast_to(sect, (DEGREES, 128))
    return jnp.asarray(np.concatenate([a, a * b, wide]).astype(np.float32))


def small_table(polar_total, azim_total):
    edge = np.arange(polar_total + 1) * (math.pi / polar_total)
    theta = (np.arange(polar_total) + 0.5) * (math.pi / polar_total)
    band = (np.cos(edge[:-1]) - np.cos(edge[1:])) * (2.0 * math.pi / azim_total)
    x = np.cos(theta)
    mean = np.zeros(polar_total)
    prev, older = np.ones_like(x), np.zeros_like(x)
    for l in range(DEGREES):
        mean[l] = azim_total * np.sum(band * prev)
        n = l + 1
        a = math.sqrt((4 * n * n - 1) / (n * n))
        b = math.sqrt(l * l / max(4 * l * l - 1, 1))
        prev, older = a * (x * prev - b * older), prev
    return jnp.asarray(np.stack([x, np.sin(theta), band, mean]).astype(np.float32))


def owner_of(sizes):
    row, ta, pa = (lax.axis_index(a) for a in AXES)
    return (row * sizes[1] + ta) * sizes[2] + pa


def stage_kernel(source, target):
    target[...] = source[...]


def pack_kernel(rho, far, shell_out, ends_out):
    rows, polar, azim = rho.shape
    ta, pa = lax.axis_index("ta"), lax.axis_index("pa")
    edge = pa * (rows - 1)
    low = ta % 2 == pa
    for k, half in enumerate((rho, far)):
        at = pl.ds(k * azim, azim)
        shell_out[:, at] = half[edge]
        for r in range(rows):
            ends_out[r : r + 1, at] = jnp.where(low, half[r, polar - 1 : polar, :], half[r, 0:1, :])


def stencil_kernel(
    sizes, rho, far, kappa, far_kappa, shell, mine, theirs, w_high, w_low, keep, send, spec, cells
):
    rows, polar, azim = rho.shape
    half = rows // 2
    row, ta, pa = (lax.axis_index(a) for a in AXES)
    low = ta % 2 == pa
    sub = lax.broadcasted_iota(jnp.int32, (polar, 2 * azim), 0)
    both = lambda a, b: jnp.concatenate([a, b], axis=1)
    at = lambda i: both(rho[i], far[i])
    turned = lambda x: both(x[:, azim:], x[:, :azim])
    outer = turned(shell[...])
    for r in range(half):
        i = pa * half + r
        c = at(i)
        if r == 0:
            ghost = jnp.where(row == 0, c, outer)
            down = jnp.where(pa == 0, ghost, at(jnp.maximum(i - 1, 0)))
        else:
            down = at(i - 1)
        if r == half - 1:
            ghost = jnp.where(row == sizes[0] - 1, c, outer)
            up = jnp.where(pa == 0, at(jnp.minimum(i + 1, rows - 1)), ghost)
        else:
            up = at(i + 1)
        near, other = mine[pl.ds(i, 1), :], turned(theirs[pl.ds(i, 1), :])
        north = jnp.where(ta == 0, turned(c[0:1, :]), jnp.where(low, other, near))
        south = jnp.where(low, near, other)
        south = jnp.where(ta == sizes[1] - 1, turned(c[polar - 1 :, :]), south)
        pol_up = jnp.where(sub == 0, north, pltpu.roll(c, 1, 0))
        pol_down = jnp.where(sub == polar - 1, south, pltpu.roll(c, polar - 1, 0))
        west = pltpu.roll(c, 1, 1)
        east = pltpu.roll(c, 2 * azim - 1, 1)
        lap = up + down + pol_up + pol_down + west + east - 6.0 * c
        new = c + both(kappa[i], far_kappa[i]) * lap
        keep[r] = new[:, :azim]
        send[r] = new[:, azim:]
        cells[r * polar : (r + 1) * polar, :] = new - 1.0
    total = None
    for k, place in enumerate((pa, 1 - pa)):
        at = pl.ds(pl.multiple_of(place * azim, azim), azim)
        term = dot3((w_high[:, at], w_low[:, at]), split(cells[:, k * azim : (k + 1) * azim]), NT)
        total = term if total is None else total + term
    spec[...] = total


def join_kernel(keep, back, out):
    half = keep.shape[0]
    pa = lax.axis_index("pa")
    out[pl.ds(pa * half, half)] = keep[...]
    out[pl.ds((1 - pa) * half, half)] = back[...]


def table_kernel(sizes, coef_ref, trig_ref, high_ref, low_ref, extra_ref, spread_ref, work):
    per, degrees, polar = work.shape
    extra_ref[...] = trig_ref[2:4, :]
    start = owner_of(sizes) * per
    lanes = 128
    order = lax.broadcasted_iota(jnp.int32, (degrees, per * lanes), 0)
    slot = lax.broadcasted_iota(jnp.int32, (degrees, per * lanes), 1) // lanes
    pick = jnp.where(order == slot + start, 1.0, 0.0).astype(F32)
    wide = lax.dot_general(
        coef_ref[: 2 * degrees, :], pick, NN,
        precision=lax.Precision.HIGHEST, preferred_element_type=F32,
    )
    for q in range(per):
        spread_ref[q] = wide[:, q * lanes : (q + 1) * lanes]
    parts = polar // lanes
    cut = lambda row, k: jnp.broadcast_to(trig_ref[row : row + 1, k * lanes : (k + 1) * lanes], (8, lanes))
    cos_t = [cut(0, k) for k in range(parts)]
    sin_t = [cut(1, k) for k in range(parts)]
    sub = lax.broadcasted_iota(jnp.int32, (8, lanes), 0)

    def block(step, carry):
        sect, prev, older = carry
        base = pl.multiple_of(step * 8, 8)
        tiles = [[jnp.zeros((8, lanes), F32)] * parts for _ in range(per)]
        for inner in range(8):
            l = base + inner
            factor = coef_ref[pl.ds(2 * degrees + l, 8, stride=0), :]
            grown = [s * (factor * sin_t[k]) for k, s in enumerate(sect)]
            if inner == 0:
                grown = [jnp.where(step == 0, s, g) for s, g in zip(sect, grown)]
            sect = grown
            fresh = []
            for q in range(per):
                a = spread_ref[q, pl.ds(l, 8, stride=0), :]
                ab = spread_ref[q, pl.ds(degrees + l, 8, stride=0), :]
                seed = l == start + q
                line = []
                for k in range(parts):
                    new = (a * cos_t[k]) * prev[q][k] - ab * older[q][k]
                    new = jnp.where(seed, sect[k], new)
                    tiles[q][k] = jnp.where(sub == inner, new, tiles[q][k])
                    line.append(new)
                fresh.append(line)
            prev, older = fresh, prev
        for q in range(per):
            for k in range(parts):
                work[q, pl.ds(base, 8), k * lanes : (k + 1) * lanes] = tiles[q][k]
        return sect, prev, older

    zero = [[jnp.zeros((8, lanes), F32)] * parts for _ in range(per)]
    lax.fori_loop(0, degrees // 8, block, ([jnp.ones((8, lanes), F32)] * parts, zero, zero))
    for q in range(per):
        at = pl.ds(q * degrees, degrees)
        high_ref[at, :], low_ref[at, :] = split(work[q])


def solve_kernel(sizes, rows, polar, spec_ref, high_ref, low_ref, extra_ref, out_ref, work_ref):
    n_row, n_ta, n_pa = sizes
    shells = rows * n_row
    pair = spec_ref.shape[1]
    per = pair // 2
    degrees = high_ref.shape[0] // per
    half = rows // n_pa
    band = extra_ref[0:1, :]
    for g in range(n_row):
        for h in range(n_pa):
            parts = [spec_ref[(g * n_ta + t) * n_pa + h] for t in range(n_ta)]
            for r in range(half):
                piece = jnp.concatenate([x[:, r * polar : (r + 1) * polar] for x in parts], axis=1)
                work_ref[pl.ds((g * rows + h * half + r) * pair, pair), :] = piece * band
    table = high_ref[...], low_ref[...]
    wide = dot3(split(work_ref[...]), table, NT)
    slot = lax.broadcasted_iota(jnp.int32, (shells * pair, degrees), 0) % per
    picked = wide[:, :degrees]
    for q in range(1, per):
        picked = jnp.where(slot == q, wide[:, q * degrees : (q + 1) * degrees], picked)
    log_eight = math.log(8.0)
    step = log_eight / shells
    degree = lax.broadcasted_iota(jnp.int32, (pair, degrees), 1).astype(F32)
    decay_in = jnp.exp(-step * degree)
    decay_out = jnp.exp(-step * (degree + 1.0))
    scale = jnp.where(degree > 0.0, -1.0 / (4.0 * math.pi * (2.0 * degree + 1.0)), 0.0)
    edges = np.exp(log_eight * (np.arange(shells + 1) / shells - 1.0))
    volume = (edges[1:] ** 3 - edges[:-1] ** 3) / 3.0
    radii = np.exp(log_eight * ((np.arange(shells) + 0.5) / shells - 1.0))
    sub = lax.broadcasted_iota(jnp.int32, (pair, degrees), 0)
    mean = jnp.where((sub == 0) & (owner_of(sizes) == 0), extra_ref[1:2, :degrees], 0.0)
    picked = [picked[i * pair : (i + 1) * pair] + mean for i in range(shells)]
    moments = [picked[i] * float(volume[i]) for i in range(shells)]
    sums = []
    carry = jnp.zeros((pair, degrees), F32)
    for i in range(shells):
        carry = carry * decay_in + moments[i]
        sums.append(carry)
    carry = jnp.zeros((pair, degrees), F32)
    for i in reversed(range(shells)):
        sums[i] = (sums[i] + carry) * (scale * float(1.0 / radii[i]))
        carry = (carry + moments[i]) * decay_out
    coeffs = jnp.concatenate(sums, axis=0)
    spread = jnp.concatenate([jnp.where(slot == q, coeffs, 0.0) for q in range(per)], axis=1)
    field = dot3(split(spread), table, NN)
    for g in range(n_row):
        for h in range(n_pa):
            for t in range(n_ta):
                pieces = []
                for r in range(half):
                    i = g * rows + h * half + r
                    pieces.append(field[i * pair : (i + 1) * pair, t * polar : (t + 1) * polar])
                out_ref[(g * n_ta + t) * n_pa + h] = jnp.concatenate(pieces, axis=1)


def potential_kernel(spec, far, w_high, w_low, out):
    rows, polar, azim = out.shape
    half = rows // 2
    pa = lax.axis_index("pa")
    at = pl.ds(pl.multiple_of(pa * azim, azim), azim)
    table = w_high[:, at], w_low[:, at]
    for part, place in ((spec, pa), (far, 1 - pa)):
        flat = dot3(split(part[...]), table, TN)
        out[pl.ds(place * half, half)] = flat.reshape(half, polar, azim)


def call(kernel, outs, specs, scratch=(), flops=0):
    shapes = tuple(jax.ShapeDtypeStruct(s, d) for s, d in outs)
    return pl.pallas_call(
        kernel,
        out_shape=shapes,
        in_specs=specs,
        out_specs=(VMEM,) * len(outs),
        scratch_shapes=list(scratch),
        compiler_params=PARAMS,
        cost_estimate=pl.CostEstimate(flops=flops, bytes_accessed=2**20, transcendentals=0),
    )


def pair_swap(value, axes, count, first):
    pairs = []
    for i in range(first, count - 1, 2):
        pairs += [(i, i + 1), (i + 1, i)]
    return lax.ppermute(value, axes, pairs)


def polar_pairs(n_ta, n_pa):
    pairs = []
    for core in range(2):
        for t in range(core, n_ta - 1, 2):
            here, there = t * n_pa + core, (t + 1) * n_pa + core
            pairs += [(here, there), (there, here)]
    return pairs


def shards(sizes, density, kappa):
    n_row, n_ta, n_pa = sizes
    rows, polar, azim = density.shape
    owners = n_row * n_ta * n_pa
    per = DEGREES // owners
    polar_total, azim_total = polar * n_ta, azim * n_pa
    half = rows // n_pa
    cells = half * polar
    swap = functools.partial(pair_swap, axes="pa", count=n_pa, first=0)

    far, far_kappa = swap(density), swap(kappa)
    (density,) = call(stage_kernel, ((density.shape, F32),), [VMEM])(density)
    (kappa,) = call(stage_kernel, ((kappa.shape, F32),), [VMEM])(kappa)
    shell, ends = call(
        pack_kernel, (((polar, azim_total), F32), ((rows, azim_total), F32)), [VMEM] * 2
    )(density, far)
    mine = lax.ppermute(ends, ("ta", "pa"), polar_pairs(n_ta, n_pa))
    shell = pair_swap(shell, ("row", "pa"), n_row * n_pa, 1)
    theirs = swap(mine)

    small = small_table(polar_total, azim_total)
    high, low, extra = call(
        functools.partial(table_kernel, sizes),
        (((per * DEGREES, polar_total), BF16),) * 2 + (((2, polar_total), F32),),
        [VMEM] * 2,
        [pltpu.VMEM((per, 2 * DEGREES, 128), F32), pltpu.VMEM((per, DEGREES, polar_total), F32)],
        flops=10**7,
    )(recursion_table(), small)

    waves = wave_table(azim_total, owners)
    keep, send, spec = call(
        functools.partial(stencil_kernel, sizes),
        (((half, polar, azim), F32), ((half, polar, azim), F32), ((2 * DEGREES, cells), F32)),
        [VMEM] * 9,
        [pltpu.VMEM((cells, azim_total), F32)],
    )(density, far, kappa, far_kappa, shell, mine, theirs, *waves)

    back = swap(send)
    spread = functools.partial(
        lax.all_to_all, axis_name=AXES, split_axis=0, concat_axis=0, tiled=True
    )
    spec = spread(spec.reshape(owners, 2 * per, cells))

    (spec,) = call(
        functools.partial(solve_kernel, sizes, rows, polar),
        ((spec.shape, F32),),
        [VMEM] * 4,
        [pltpu.VMEM((rows * n_row * 2 * per, polar_total), F32)],
    )(spec, high, low, extra)
    spec = spread(spec).reshape(2 * DEGREES, cells)
    far = swap(spec)
    (updated,) = call(join_kernel, ((density.shape, F32),), [VMEM] * 2)(keep, back)
    (potential,) = call(potential_kernel, ((density.shape, F32),), [VMEM] * 4)(spec, far, *waves)
    return (updated, potential)


def solution(mesh):
    sizes = tuple(mesh.shape[a] for a in AXES)
    placed = (P(*AXES), P(*AXES))

    def body(density, kappa):
        return shards(sizes, density, kappa)

    return jax.shard_map(body, mesh=mesh, in_specs=placed, out_specs=placed, check_vma=False)
```

```python
import functools
import math

import jax
import jax.numpy as jnp
import numpy as np
from jax import lax
from jax.experimental import pallas as pl
from jax.experimental.pallas import tpu as pltpu
from jax.sharding import PartitionSpec as P


DEGREES = 128
AXES = ("row", "ta", "pa")
VMEM = pl.BlockSpec(memory_space=pltpu.VMEM)
PARAMS = pltpu.CompilerParams(vmem_limit_bytes=16 * 2**20)
F32 = jnp.float32
BF16 = jnp.bfloat16
NT = (((1,), (1,)), ((), ()))
NN = (((1,), (0,)), ((), ()))
TN = (((0,), (0,)), ((), ()))


def split(x):
    high = x.astype(BF16)
    return high, (x - high.astype(F32)).astype(BF16)


def dot3(a, b, dims):
    one = functools.partial(lax.dot_general, dimension_numbers=dims, preferred_element_type=F32)
    return one(a[0], b[0]) + (one(a[0], b[1]) + one(a[1], b[0]))


def wave_table(azim_total, owners):
    modes = np.arange(DEGREES).reshape(owners, 1, -1, 1)
    phi = (np.arange(azim_total) + 0.5) * (2.0 * math.pi / azim_total)
    both = np.concatenate([np.cos(modes * phi), np.sin(modes * phi)], axis=1)
    table = both.reshape(2 * DEGREES, azim_total)
    high = table.astype(BF16)
    low = (table - high.astype(np.float64)).astype(BF16)
    return jnp.asarray(high), jnp.asarray(low)


def recursion_table():
    l = np.arange(DEGREES, dtype=np.float64)[:, None]
    m = np.arange(DEGREES, dtype=np.float64)[None, :]
    below = m < l
    a = np.sqrt((4 * l * l - 1) / np.where(below, l * l - m * m, 1.0) * below)
    low = l - 1
    b = np.sqrt(np.maximum(low * low - m * m, 0) / np.maximum(4 * low * low - 1, 1.0))
    sect = np.where(l == 1, math.sqrt(3.0), np.sqrt((2 * l + 1) / np.maximum(2 * l, 1.0)))
    wide = np.broadcast_to(sect, (DEGREES, 128))
    return jnp.asarray(np.concatenate([a, a * b, wide]).astype(np.float32))


def small_table(polar_total, azim_total):
    edge = np.arange(polar_total + 1) * (math.pi / polar_total)
    theta = (np.arange(polar_total) + 0.5) * (math.pi / polar_total)
    band = (np.cos(edge[:-1]) - np.cos(edge[1:])) * (2.0 * math.pi / azim_total)
    x = np.cos(theta)
    mean = np.zeros(polar_total)
    prev, older = np.ones_like(x), np.zeros_like(x)
    for l in range(DEGREES):
        mean[l] = azim_total * np.sum(band * prev)
        n = l + 1
        a = math.sqrt((4 * n * n - 1) / (n * n))
        b = math.sqrt(l * l / max(4 * l * l - 1, 1))
        prev, older = a * (x * prev - b * older), prev
    return jnp.asarray(np.stack([x, np.sin(theta), band, mean]).astype(np.float32))


def owner_of(sizes):
    row, ta, pa = (lax.axis_index(a) for a in AXES)
    return (row * sizes[1] + ta) * sizes[2] + pa


def stage_kernel(source, target):
    target[...] = source[...]


def pack_kernel(rho, far, shell_out, ends_out):
    rows, polar, azim = rho.shape
    ta, pa = lax.axis_index("ta"), lax.axis_index("pa")
    edge = pa * (rows - 1)
    low = ta % 2 == pa
    for k, half in enumerate((rho, far)):
        at = pl.ds(k * azim, azim)
        shell_out[:, at] = half[edge]
        for r in range(rows):
            ends_out[r : r + 1, at] = jnp.where(low, half[r, polar - 1 : polar, :], half[r, 0:1, :])


def stencil_kernel(
    sizes, rho, far, kappa, far_kappa, shell, mine, theirs, w_high, w_low, keep, send, spec, cells
):
    rows, polar, azim = rho.shape
    half = rows // 2
    row, ta, pa = (lax.axis_index(a) for a in AXES)
    low = ta % 2 == pa
    sub = lax.broadcasted_iota(jnp.int32, (polar, 2 * azim), 0)
    both = lambda a, b: jnp.concatenate([a, b], axis=1)
    at = lambda i: both(rho[i], far[i])
    turned = lambda x: both(x[:, azim:], x[:, :azim])
    outer = turned(shell[...])
    for r in range(half):
        i = pa * half + r
        c = at(i)
        if r == 0:
            ghost = jnp.where(row == 0, c, outer)
            down = jnp.where(pa == 0, ghost, at(jnp.maximum(i - 1, 0)))
        else:
            down = at(i - 1)
        if r == half - 1:
            ghost = jnp.where(row == sizes[0] - 1, c, outer)
            up = jnp.where(pa == 0, at(jnp.minimum(i + 1, rows - 1)), ghost)
        else:
            up = at(i + 1)
        near, other = mine[pl.ds(i, 1), :], turned(theirs[pl.ds(i, 1), :])
        north = jnp.where(ta == 0, turned(c[0:1, :]), jnp.where(low, other, near))
        south = jnp.where(low, near, other)
        south = jnp.where(ta == sizes[1] - 1, turned(c[polar - 1 :, :]), south)
        pol_up = jnp.where(sub == 0, north, pltpu.roll(c, 1, 0))
        pol_down = jnp.where(sub == polar - 1, south, pltpu.roll(c, polar - 1, 0))
        west = pltpu.roll(c, 1, 1)
        east = pltpu.roll(c, 2 * azim - 1, 1)
        lap = up + down + pol_up + pol_down + west + east - 6.0 * c
        new = c + both(kappa[i], far_kappa[i]) * lap
        keep[r] = new[:, :azim]
        send[r] = new[:, azim:]
        cells[r * polar : (r + 1) * polar, :] = new - 1.0
    total = None
    for k, place in enumerate((pa, 1 - pa)):
        at = pl.ds(pl.multiple_of(place * azim, azim), azim)
        term = dot3((w_high[:, at], w_low[:, at]), split(cells[:, k * azim : (k + 1) * azim]), NT)
        total = term if total is None else total + term
    spec[...] = total


def join_kernel(keep, back, out):
    half = keep.shape[0]
    pa = lax.axis_index("pa")
    out[pl.ds(pa * half, half)] = keep[...]
    out[pl.ds((1 - pa) * half, half)] = back[...]


def table_kernel(sizes, coef_ref, trig_ref, high_ref, low_ref, extra_ref, spread_ref, work):
    per, degrees, polar = work.shape
    extra_ref[...] = trig_ref[2:4, :]
    start = owner_of(sizes) * per
    lanes = 128
    order = lax.broadcasted_iota(jnp.int32, (degrees, per * lanes), 0)
    slot = lax.broadcasted_iota(jnp.int32, (degrees, per * lanes), 1) // lanes
    pick = jnp.where(order == slot + start, 1.0, 0.0).astype(F32)
    wide = lax.dot_general(
        coef_ref[: 2 * degrees, :], pick, NN,
        precision=lax.Precision.HIGHEST, preferred_element_type=F32,
    )
    for q in range(per):
        spread_ref[q] = wide[:, q * lanes : (q + 1) * lanes]
    parts = polar // lanes
    cut = lambda row, k: jnp.broadcast_to(trig_ref[row : row + 1, k * lanes : (k + 1) * lanes], (8, lanes))
    cos_t = [cut(0, k) for k in range(parts)]
    sin_t = [cut(1, k) for k in range(parts)]
    sub = lax.broadcasted_iota(jnp.int32, (8, lanes), 0)

    def block(step, carry):
        sect, prev, older = carry
        base = pl.multiple_of(step * 8, 8)
        tiles = [[jnp.zeros((8, lanes), F32)] * parts for _ in range(per)]
        for inner in range(8):
            l = base + inner
            factor = coef_ref[pl.ds(2 * degrees + l, 8, stride=0), :]
            grown = [s * (factor * sin_t[k]) for k, s in enumerate(sect)]
            if inner == 0:
                grown = [jnp.where(step == 0, s, g) for s, g in zip(sect, grown)]
            sect = grown
            fresh = []
            for q in range(per):
                a = spread_ref[q, pl.ds(l, 8, stride=0), :]
                ab = spread_ref[q, pl.ds(degrees + l, 8, stride=0), :]
                seed = l == start + q
                line = []
                for k in range(parts):
                    new = (a * cos_t[k]) * prev[q][k] - ab * older[q][k]
                    new = jnp.where(seed, sect[k], new)
                    tiles[q][k] = jnp.where(sub == inner, new, tiles[q][k])
                    line.append(new)
                fresh.append(line)
            prev, older = fresh, prev
        for q in range(per):
            for k in range(parts):
                work[q, pl.ds(base, 8), k * lanes : (k + 1) * lanes] = tiles[q][k]
        return sect, prev, older

    zero = [[jnp.zeros((8, lanes), F32)] * parts for _ in range(per)]
    lax.fori_loop(0, degrees // 8, block, ([jnp.ones((8, lanes), F32)] * parts, zero, zero))
    for q in range(per):
        at = pl.ds(q * degrees, degrees)
        high_ref[at, :], low_ref[at, :] = split(work[q])


def solve_kernel(sizes, rows, polar, spec_ref, high_ref, low_ref, extra_ref, out_ref, work_ref):
    n_row, n_ta, n_pa = sizes
    shells = rows * n_row
    pair = spec_ref.shape[1]
    per = pair // 2
    degrees = high_ref.shape[0] // per
    half = rows // n_pa
    band = extra_ref[0:1, :]
    for g in range(n_row):
        for h in range(n_pa):
            parts = [spec_ref[(g * n_ta + t) * n_pa + h] for t in range(n_ta)]
            for r in range(half):
                piece = jnp.concatenate([x[:, r * polar : (r + 1) * polar] for x in parts], axis=1)
                work_ref[pl.ds((g * rows + h * half + r) * pair, pair), :] = piece * band
    table = high_ref[...], low_ref[...]
    wide = dot3(split(work_ref[...]), table, NT)
    slot = lax.broadcasted_iota(jnp.int32, (shells * pair, degrees), 0) % per
    picked = wide[:, :degrees]
    for q in range(1, per):
        picked = jnp.where(slot == q, wide[:, q * degrees : (q + 1) * degrees], picked)
    log_eight = math.log(8.0)
    step = log_eight / shells
    degree = lax.broadcasted_iota(jnp.int32, (pair, degrees), 1).astype(F32)
    decay_in = jnp.exp(-step * degree)
    decay_out = jnp.exp(-step * (degree + 1.0))
    scale = jnp.where(degree > 0.0, -1.0 / (4.0 * math.pi * (2.0 * degree + 1.0)), 0.0)
    edges = np.exp(log_eight * (np.arange(shells + 1) / shells - 1.0))
    volume = (edges[1:] ** 3 - edges[:-1] ** 3) / 3.0
    radii = np.exp(log_eight * ((np.arange(shells) + 0.5) / shells - 1.0))
    sub = lax.broadcasted_iota(jnp.int32, (pair, degrees), 0)
    mean = jnp.where((sub == 0) & (owner_of(sizes) == 0), extra_ref[1:2, :degrees], 0.0)
    picked = [picked[i * pair : (i + 1) * pair] + mean for i in range(shells)]
    moments = [picked[i] * float(volume[i]) for i in range(shells)]
    sums = []
    carry = jnp.zeros((pair, degrees), F32)
    for i in range(shells):
        carry = carry * decay_in + moments[i]
        sums.append(carry)
    carry = jnp.zeros((pair, degrees), F32)
    for i in reversed(range(shells)):
        sums[i] = (sums[i] + carry) * (scale * float(1.0 / radii[i]))
        carry = (carry + moments[i]) * decay_out
    coeffs = jnp.concatenate(sums, axis=0)
    spread = jnp.concatenate([jnp.where(slot == q, coeffs, 0.0) for q in range(per)], axis=1)
    field = dot3(split(spread), table, NN)
    for g in range(n_row):
        for h in range(n_pa):
            for t in range(n_ta):
                pieces = []
                for r in range(half):
                    i = g * rows + h * half + r
                    pieces.append(field[i * pair : (i + 1) * pair, t * polar : (t + 1) * polar])
                out_ref[(g * n_ta + t) * n_pa + h] = jnp.concatenate(pieces, axis=1)


def potential_kernel(spec, far, w_high, w_low, out):
    rows, polar, azim = out.shape
    half = rows // 2
    pa = lax.axis_index("pa")
    at = pl.ds(pl.multiple_of(pa * azim, azim), azim)
    table = w_high[:, at], w_low[:, at]
    for part, place in ((spec, pa), (far, 1 - pa)):
        flat = dot3(split(part[...]), table, TN)
        out[pl.ds(place * half, half)] = flat.reshape(half, polar, azim)


def call(kernel, outs, specs, scratch=(), flops=0):
    shapes = tuple(jax.ShapeDtypeStruct(s, d) for s, d in outs)
    return pl.pallas_call(
        kernel,
        out_shape=shapes,
        in_specs=specs,
        out_specs=(VMEM,) * len(outs),
        scratch_shapes=list(scratch),
        compiler_params=PARAMS,
        cost_estimate=pl.CostEstimate(flops=flops, bytes_accessed=2**20, transcendentals=0),
    )


def pair_swap(value, axes, count, first):
    pairs = []
    for i in range(first, count - 1, 2):
        pairs += [(i, i + 1), (i + 1, i)]
    return lax.ppermute(value, axes, pairs)


def halo_pairs(sizes, partner, spare):
    _, n_ta, n_pa = sizes
    number = lambda place: (place[0] * n_ta + place[1]) * n_pa + place[2]
    inside = lambda place: all(0 <= x < n for x, n in zip(place, sizes))
    pairs = []
    for place in np.ndindex(*sizes):
        other = partner(*place)
        if not inside(other):
            other = spare(*place)
        if inside(other):
            pairs.append((number(place), number(other)))
    return pairs


def radial_partner(row, ta, pa):
    return (row + 1, ta, 0) if pa == 1 else (row - 1, ta, 1)


def polar_partner(row, ta, pa):
    return (row, ta + 1 if ta % 2 == pa else ta - 1, pa)


def shards(sizes, density, kappa):
    n_row, n_ta, n_pa = sizes
    rows, polar, azim = density.shape
    owners = n_row * n_ta * n_pa
    per = DEGREES // owners
    polar_total, azim_total = polar * n_ta, azim * n_pa
    half = rows // n_pa
    cells = half * polar
    swap = functools.partial(pair_swap, axes="pa", count=n_pa, first=0)

    far, far_kappa = swap(density), swap(kappa)
    (density,) = call(stage_kernel, ((density.shape, F32),), [VMEM])(density)
    (kappa,) = call(stage_kernel, ((kappa.shape, F32),), [VMEM])(kappa)
    shell, ends = call(
        pack_kernel, (((polar, azim_total), F32), ((rows, azim_total), F32)), [VMEM] * 2
    )(density, far)
    pairs = halo_pairs(sizes, polar_partner, lambda row, ta, pa: (row ^ 1, ta, pa))
    mine = lax.ppermute(ends, AXES, pairs)
    pairs = halo_pairs(sizes, radial_partner, lambda row, ta, pa: (row, ta ^ 1, pa))
    shell = lax.ppermute(shell, AXES, pairs)
    theirs = swap(mine)

    small = small_table(polar_total, azim_total)
    high, low, extra = call(
        functools.partial(table_kernel, sizes),
        (((per * DEGREES, polar_total), BF16),) * 2 + (((2, polar_total), F32),),
        [VMEM] * 2,
        [pltpu.VMEM((per, 2 * DEGREES, 128), F32), pltpu.VMEM((per, DEGREES, polar_total), F32)],
        flops=10**7,
    )(recursion_table(), small)

    waves = wave_table(azim_total, owners)
    keep, send, spec = call(
        functools.partial(stencil_kernel, sizes),
        (((half, polar, azim), F32), ((half, polar, azim), F32), ((2 * DEGREES, cells), F32)),
        [VMEM] * 9,
        [pltpu.VMEM((cells, azim_total), F32)],
    )(density, far, kappa, far_kappa, shell, mine, theirs, *waves)

    back = swap(send)
    spread = functools.partial(
        lax.all_to_all, axis_name=AXES, split_axis=0, concat_axis=0, tiled=True
    )
    spec = spread(spec.reshape(owners, 2 * per, cells))

    (spec,) = call(
        functools.partial(solve_kernel, sizes, rows, polar),
        ((spec.shape, F32),),
        [VMEM] * 4,
        [pltpu.VMEM((rows * n_row * 2 * per, polar_total), F32)],
    )(spec, high, low, extra)
    spec = spread(spec).reshape(2 * DEGREES, cells)
    far = swap(spec)
    (updated,) = call(join_kernel, ((density.shape, F32),), [VMEM] * 2)(keep, back)
    (potential,) = call(potential_kernel, ((density.shape, F32),), [VMEM] * 4)(spec, far, *waves)
    return (updated, potential)


def solution(mesh):
    sizes = tuple(mesh.shape[a] for a in AXES)
    placed = (P(*AXES), P(*AXES))

    def body(density, kappa):
        return shards(sizes, density, kappa)

    return jax.shard_map(body, mesh=mesh, in_specs=placed, out_specs=placed, check_vma=False)
```

```python
import functools
import math

import jax
import jax.numpy as jnp
import numpy as np
from jax import lax
from jax.experimental import pallas as pl
from jax.experimental.pallas import tpu as pltpu
from jax.sharding import PartitionSpec as P


DEGREES = 128
AXES = ("row", "ta", "pa")
VMEM = pl.BlockSpec(memory_space=pltpu.VMEM)
PARAMS = pltpu.CompilerParams(vmem_limit_bytes=16 * 2**20)
F32 = jnp.float32
BF16 = jnp.bfloat16
NT = (((1,), (1,)), ((), ()))
NN = (((1,), (0,)), ((), ()))
TN = (((0,), (0,)), ((), ()))


def split(x):
    high = x.astype(BF16)
    return high, (x - high.astype(F32)).astype(BF16)


def dot3(a, b, dims):
    one = functools.partial(lax.dot_general, dimension_numbers=dims, preferred_element_type=F32)
    return one(a[0], b[0]) + (one(a[0], b[1]) + one(a[1], b[0]))


def wave_table(azim_total, owners):
    modes = np.arange(DEGREES).reshape(owners, 1, -1, 1)
    phi = (np.arange(azim_total) + 0.5) * (2.0 * math.pi / azim_total)
    both = np.concatenate([np.cos(modes * phi), np.sin(modes * phi)], axis=1)
    table = both.reshape(2 * DEGREES, azim_total)
    high = table.astype(BF16)
    low = (table - high.astype(np.float64)).astype(BF16)
    return jnp.asarray(high), jnp.asarray(low)


def recursion_table():
    l = np.arange(DEGREES, dtype=np.float64)[:, None]
    m = np.arange(DEGREES, dtype=np.float64)[None, :]
    below = m < l
    a = np.sqrt((4 * l * l - 1) / np.where(below, l * l - m * m, 1.0) * below)
    low = l - 1
    b = np.sqrt(np.maximum(low * low - m * m, 0) / np.maximum(4 * low * low - 1, 1.0))
    sect = np.where(l == 1, math.sqrt(3.0), np.sqrt((2 * l + 1) / np.maximum(2 * l, 1.0)))
    wide = np.broadcast_to(sect, (DEGREES, 128))
    return jnp.asarray(np.concatenate([a, a * b, wide]).astype(np.float32))


def small_table(polar_total, azim_total):
    edge = np.arange(polar_total + 1) * (math.pi / polar_total)
    theta = (np.arange(polar_total) + 0.5) * (math.pi / polar_total)
    band = (np.cos(edge[:-1]) - np.cos(edge[1:])) * (2.0 * math.pi / azim_total)
    x = np.cos(theta)
    mean = np.zeros(polar_total)
    prev, older = np.ones_like(x), np.zeros_like(x)
    for l in range(DEGREES):
        mean[l] = azim_total * np.sum(band * prev)
        n = l + 1
        a = math.sqrt((4 * n * n - 1) / (n * n))
        b = math.sqrt(l * l / max(4 * l * l - 1, 1))
        prev, older = a * (x * prev - b * older), prev
    return jnp.asarray(np.stack([x, np.sin(theta), band, mean]).astype(np.float32))


def owner_of(sizes):
    row, ta, pa = (lax.axis_index(a) for a in AXES)
    return (row * sizes[1] + ta) * sizes[2] + pa


def stage_kernel(source, target):
    target[...] = source[...]


def pack_kernel(rho, far, shell_out, ends_out):
    rows, polar, azim = rho.shape
    ta, pa = lax.axis_index("ta"), lax.axis_index("pa")
    edge = pa * (rows - 1)
    low = ta % 2 == pa
    for k, half in enumerate((rho, far)):
        at = pl.ds(k * azim, azim)
        shell_out[:, at] = half[edge]
        for r in range(rows):
            ends_out[r : r + 1, at] = jnp.where(low, half[r, polar - 1 : polar, :], half[r, 0:1, :])


def stencil_kernel(
    sizes, rho, far, kappa, far_kappa, shell, mine, theirs, w_high, w_low, keep, send, spec, cells
):
    rows, polar, azim = rho.shape
    half = rows // 2
    row, ta, pa = (lax.axis_index(a) for a in AXES)
    low = ta % 2 == pa
    sub = lax.broadcasted_iota(jnp.int32, (polar, 2 * azim), 0)
    both = lambda a, b: jnp.concatenate([a, b], axis=1)
    at = lambda i: both(rho[i], far[i])
    turned = lambda x: both(x[:, azim:], x[:, :azim])
    outer = turned(shell[...])
    for r in range(half):
        i = pa * half + r
        c = at(i)
        if r == 0:
            ghost = jnp.where(row == 0, c, outer)
            down = jnp.where(pa == 0, ghost, at(jnp.maximum(i - 1, 0)))
        else:
            down = at(i - 1)
        if r == half - 1:
            ghost = jnp.where(row == sizes[0] - 1, c, outer)
            up = jnp.where(pa == 0, at(jnp.minimum(i + 1, rows - 1)), ghost)
        else:
            up = at(i + 1)
        near, other = mine[pl.ds(i, 1), :], turned(theirs[pl.ds(i, 1), :])
        north = jnp.where(ta == 0, turned(c[0:1, :]), jnp.where(low, other, near))
        south = jnp.where(low, near, other)
        south = jnp.where(ta == sizes[1] - 1, turned(c[polar - 1 :, :]), south)
        pol_up = jnp.where(sub == 0, north, pltpu.roll(c, 1, 0))
        pol_down = jnp.where(sub == polar - 1, south, pltpu.roll(c, polar - 1, 0))
        west = pltpu.roll(c, 1, 1)
        east = pltpu.roll(c, 2 * azim - 1, 1)
        lap = up + down + pol_up + pol_down + west + east - 6.0 * c
        new = c + both(kappa[i], far_kappa[i]) * lap
        keep[r] = new[:, :azim]
        send[r] = new[:, azim:]
        cells[r * polar : (r + 1) * polar, :] = new - 1.0
    total = None
    for k, place in enumerate((pa, 1 - pa)):
        at = pl.ds(pl.multiple_of(place * azim, azim), azim)
        term = dot3((w_high[:, at], w_low[:, at]), split(cells[:, k * azim : (k + 1) * azim]), NT)
        total = term if total is None else total + term
    spec[...] = total


def join_kernel(keep, back, out):
    half = keep.shape[0]
    pa = lax.axis_index("pa")
    out[pl.ds(pa * half, half)] = keep[...]
    out[pl.ds((1 - pa) * half, half)] = back[...]


def table_kernel(sizes, coef_ref, trig_ref, high_ref, low_ref, extra_ref, spread_ref, work):
    per, degrees, north = work.shape
    extra_ref[...] = trig_ref[2:4, :]
    start = owner_of(sizes) * per
    lanes = 128
    near = pltpu.roll(coef_ref[: 2 * degrees, :], lanes - start, 1)
    for q in range(per):
        spread_ref[q] = jnp.broadcast_to(near[:, q : q + 1], (2 * degrees, lanes))
    parts = north // lanes
    cut = lambda row, k: jnp.broadcast_to(trig_ref[row : row + 1, k * lanes : (k + 1) * lanes], (8, lanes))
    cos_t = [cut(0, k) for k in range(parts)]
    sin_t = [cut(1, k) for k in range(parts)]
    sub = lax.broadcasted_iota(jnp.int32, (8, lanes), 0)

    def block(step, carry):
        sect, prev, older = carry
        base = pl.multiple_of(step * 8, 8)
        tiles = [[jnp.zeros((8, lanes), F32)] * parts for _ in range(per)]
        for inner in range(8):
            l = base + inner
            factor = coef_ref[pl.ds(2 * degrees + l, 8, stride=0), :]
            grown = [s * (factor * sin_t[k]) for k, s in enumerate(sect)]
            if inner == 0:
                grown = [jnp.where(step == 0, s, g) for s, g in zip(sect, grown)]
            sect = grown
            fresh = []
            for q in range(per):
                a = spread_ref[q, pl.ds(l, 8, stride=0), :]
                ab = spread_ref[q, pl.ds(degrees + l, 8, stride=0), :]
                seed = l == start + q
                line = []
                for k in range(parts):
                    rest = jnp.where(seed, sect[k], 0.0) - ab * older[q][k]
                    new = (a * cos_t[k]) * prev[q][k] + rest
                    tiles[q][k] = jnp.where(sub == inner, new, tiles[q][k])
                    line.append(new)
                fresh.append(line)
            prev, older = fresh, prev
        for q in range(per):
            for k in range(parts):
                work[q, pl.ds(base, 8), k * lanes : (k + 1) * lanes] = tiles[q][k]
        return sect, prev, older

    zero = [[jnp.zeros((8, lanes), F32)] * parts for _ in range(per)]
    lax.fori_loop(0, degrees // 8, block, ([jnp.ones((8, lanes), F32)] * parts, zero, zero))
    square = lambda d: lax.broadcasted_iota(jnp.int32, (north, north), d)
    mirror = jnp.where(square(0) + square(1) == north - 1, 1.0, 0.0).astype(BF16)
    line = lax.broadcasted_iota(jnp.int32, (per * degrees, north), 0)
    sign = jnp.where((line + line // degrees + start) % 2 == 0, 1.0, -1.0)
    for piece, ref in zip(split(work[...].reshape(per * degrees, north)), (high_ref, low_ref)):
        ref[:, :north] = piece
        flipped = lax.dot_general(piece, mirror, NN, preferred_element_type=F32)
        ref[:, north:] = (sign * flipped).astype(BF16)


def solve_kernel(sizes, rows, polar, spec_ref, high_ref, low_ref, extra_ref, out_ref, work_ref):
    n_row, n_ta, n_pa = sizes
    shells = rows * n_row
    pair = spec_ref.shape[1]
    per = pair // 2
    degrees = high_ref.shape[0] // per
    half = rows // n_pa
    band = extra_ref[0:1, :]
    for g in range(n_row):
        for h in range(n_pa):
            parts = [spec_ref[(g * n_ta + t) * n_pa + h] for t in range(n_ta)]
            for r in range(half):
                piece = jnp.concatenate([x[:, r * polar : (r + 1) * polar] for x in parts], axis=1)
                work_ref[pl.ds((g * rows + h * half + r) * pair, pair), :] = piece * band
    table = high_ref[...], low_ref[...]
    wide = dot3(split(work_ref[...]), table, NT)
    slot = lax.broadcasted_iota(jnp.int32, (shells * pair, degrees), 0) % per
    picked = wide[:, :degrees]
    for q in range(1, per):
        picked = jnp.where(slot == q, wide[:, q * degrees : (q + 1) * degrees], picked)
    log_eight = math.log(8.0)
    step = log_eight / shells
    degree = lax.broadcasted_iota(jnp.int32, (pair, degrees), 1).astype(F32)
    decay_in = jnp.exp(-step * degree)
    decay_out = jnp.exp(-step * (degree + 1.0))
    scale = jnp.where(degree > 0.0, -1.0 / (4.0 * math.pi * (2.0 * degree + 1.0)), 0.0)
    edges = np.exp(log_eight * (np.arange(shells + 1) / shells - 1.0))
    volume = (edges[1:] ** 3 - edges[:-1] ** 3) / 3.0
    radii = np.exp(log_eight * ((np.arange(shells) + 0.5) / shells - 1.0))
    sub = lax.broadcasted_iota(jnp.int32, (pair, degrees), 0)
    mean = jnp.where((sub == 0) & (owner_of(sizes) == 0), extra_ref[1:2, :degrees], 0.0)
    picked = [picked[i * pair : (i + 1) * pair] + mean for i in range(shells)]
    moments = [picked[i] * float(volume[i]) for i in range(shells)]
    sums = []
    carry = jnp.zeros((pair, degrees), F32)
    for i in range(shells):
        carry = carry * decay_in + moments[i]
        sums.append(carry)
    carry = jnp.zeros((pair, degrees), F32)
    for i in reversed(range(shells)):
        sums[i] = (sums[i] + carry) * (scale * float(1.0 / radii[i]))
        carry = (carry + moments[i]) * decay_out
    coeffs = jnp.concatenate(sums, axis=0)
    spread = jnp.concatenate([jnp.where(slot == q, coeffs, 0.0) for q in range(per)], axis=1)
    field = dot3(split(spread), table, NN)
    for g in range(n_row):
        for h in range(n_pa):
            for t in range(n_ta):
                pieces = []
                for r in range(half):
                    i = g * rows + h * half + r
                    pieces.append(field[i * pair : (i + 1) * pair, t * polar : (t + 1) * polar])
                out_ref[(g * n_ta + t) * n_pa + h] = jnp.concatenate(pieces, axis=1)


def potential_kernel(spec, far, w_high, w_low, out):
    rows, polar, azim = out.shape
    half = rows // 2
    pa = lax.axis_index("pa")
    at = pl.ds(pl.multiple_of(pa * azim, azim), azim)
    table = w_high[:, at], w_low[:, at]
    for part, place in ((spec, pa), (far, 1 - pa)):
        flat = dot3(split(part[...]), table, TN)
        out[pl.ds(place * half, half)] = flat.reshape(half, polar, azim)


def call(kernel, outs, specs, scratch=(), flops=0):
    shapes = tuple(jax.ShapeDtypeStruct(s, d) for s, d in outs)
    return pl.pallas_call(
        kernel,
        out_shape=shapes,
        in_specs=specs,
        out_specs=(VMEM,) * len(outs),
        scratch_shapes=list(scratch),
        compiler_params=PARAMS,
        cost_estimate=pl.CostEstimate(flops=flops, bytes_accessed=2**20, transcendentals=0),
    )


def pair_swap(value, axes, count, first):
    pairs = []
    for i in range(first, count - 1, 2):
        pairs += [(i, i + 1), (i + 1, i)]
    return lax.ppermute(value, axes, pairs)


def halo_pairs(sizes, partner, spare):
    _, n_ta, n_pa = sizes
    number = lambda place: (place[0] * n_ta + place[1]) * n_pa + place[2]
    inside = lambda place: all(0 <= x < n for x, n in zip(place, sizes))
    pairs = []
    for place in np.ndindex(*sizes):
        other = partner(*place)
        if not inside(other):
            other = spare(*place)
        if inside(other):
            pairs.append((number(place), number(other)))
    return pairs


def radial_partner(row, ta, pa):
    return (row + 1, ta, 0) if pa == 1 else (row - 1, ta, 1)


def polar_partner(row, ta, pa):
    return (row, ta + 1 if ta % 2 == pa else ta - 1, pa)


def shards(sizes, density, kappa):
    n_row, n_ta, n_pa = sizes
    rows, polar, azim = density.shape
    owners = n_row * n_ta * n_pa
    per = DEGREES // owners
    polar_total, azim_total = polar * n_ta, azim * n_pa
    half = rows // n_pa
    cells = half * polar
    swap = functools.partial(pair_swap, axes="pa", count=n_pa, first=0)

    far, far_kappa = swap(density), swap(kappa)
    (density,) = call(stage_kernel, ((density.shape, F32),), [VMEM])(density)
    (kappa,) = call(stage_kernel, ((kappa.shape, F32),), [VMEM])(kappa)
    shell, ends = call(
        pack_kernel, (((polar, azim_total), F32), ((rows, azim_total), F32)), [VMEM] * 2
    )(density, far)
    pairs = halo_pairs(sizes, polar_partner, lambda row, ta, pa: (row ^ 1, ta, pa))
    mine = lax.ppermute(ends, AXES, pairs)
    pairs = halo_pairs(sizes, radial_partner, lambda row, ta, pa: (row, ta ^ 1, pa))
    shell = lax.ppermute(shell, AXES, pairs)
    theirs = swap(mine)

    small = small_table(polar_total, azim_total)
    high, low, extra = call(
        functools.partial(table_kernel, sizes),
        (((per * DEGREES, polar_total), BF16),) * 2 + (((2, polar_total), F32),),
        [VMEM] * 2,
        [pltpu.VMEM((per, 2 * DEGREES, 128), F32), pltpu.VMEM((per, DEGREES, polar_total // 2), F32)],
        flops=10**7,
    )(recursion_table(), small)

    waves = wave_table(azim_total, owners)
    keep, send, spec = call(
        functools.partial(stencil_kernel, sizes),
        (((half, polar, azim), F32), ((half, polar, azim), F32), ((2 * DEGREES, cells), F32)),
        [VMEM] * 9,
        [pltpu.VMEM((cells, azim_total), F32)],
    )(density, far, kappa, far_kappa, shell, mine, theirs, *waves)

    back = swap(send)
    spread = functools.partial(
        lax.all_to_all, axis_name=AXES, split_axis=0, concat_axis=0, tiled=True
    )
    spec = spread(spec.reshape(owners, 2 * per, cells))

    (spec,) = call(
        functools.partial(solve_kernel, sizes, rows, polar),
        ((spec.shape, F32),),
        [VMEM] * 4,
        [pltpu.VMEM((rows * n_row * 2 * per, polar_total), F32)],
    )(spec, high, low, extra)
    spec = spread(spec).reshape(2 * DEGREES, cells)
    far = swap(spec)
    (updated,) = call(join_kernel, ((density.shape, F32),), [VMEM] * 2)(keep, back)
    (potential,) = call(potential_kernel, ((density.shape, F32),), [VMEM] * 4)(spec, far, *waves)
    return (updated, potential)


def solution(mesh):
    sizes = tuple(mesh.shape[a] for a in AXES)
    placed = (P(*AXES), P(*AXES))

    def body(density, kappa):
        return shards(sizes, density, kappa)

    return jax.shard_map(body, mesh=mesh, in_specs=placed, out_specs=placed, check_vma=False)
```

```python
import functools
import math

import jax
import jax.numpy as jnp
import numpy as np
from jax import lax
from jax.experimental import pallas as pl
from jax.experimental.pallas import tpu as pltpu
from jax.sharding import PartitionSpec as P


DEGREES = 128
AXES = ("row", "ta", "pa")
VMEM = pl.BlockSpec(memory_space=pltpu.VMEM)
PARAMS = pltpu.CompilerParams(vmem_limit_bytes=16 * 2**20)
F32 = jnp.float32
BF16 = jnp.bfloat16
NT = (((1,), (1,)), ((), ()))
NN = (((1,), (0,)), ((), ()))
TN = (((0,), (0,)), ((), ()))


def split(x):
    high = x.astype(BF16)
    return high, (x - high.astype(F32)).astype(BF16)


def dot3(a, b, dims):
    one = functools.partial(lax.dot_general, dimension_numbers=dims, preferred_element_type=F32)
    axis = 1 - dims[0][0][0]
    rows = a[0].shape[axis]
    wide = one(jnp.concatenate(a, axis=axis), b[0])
    return wide[:rows] + (wide[rows:] + one(a[0], b[1]))


def wave_table(azim_total, owners):
    modes = np.arange(DEGREES).reshape(owners, 1, -1, 1)
    phi = (np.arange(azim_total) + 0.5) * (2.0 * math.pi / azim_total)
    both = np.concatenate([np.cos(modes * phi), np.sin(modes * phi)], axis=1)
    table = both.reshape(2 * DEGREES, azim_total)
    high = table.astype(BF16)
    low = (table - high.astype(np.float64)).astype(BF16)
    return jnp.asarray(high), jnp.asarray(low)


def recursion_table():
    l = np.arange(DEGREES, dtype=np.float64)[:, None]
    m = np.arange(DEGREES, dtype=np.float64)[None, :]
    below = m < l
    a = np.sqrt((4 * l * l - 1) / np.where(below, l * l - m * m, 1.0) * below)
    low = l - 1
    b = np.sqrt(np.maximum(low * low - m * m, 0) / np.maximum(4 * low * low - 1, 1.0))
    sect = np.where(l == 1, math.sqrt(3.0), np.sqrt((2 * l + 1) / np.maximum(2 * l, 1.0)))
    wide = np.broadcast_to(sect, (DEGREES, 128))
    return jnp.asarray(np.concatenate([a, a * b, wide]).astype(np.float32))


def small_table(polar_total, azim_total):
    edge = np.arange(polar_total + 1) * (math.pi / polar_total)
    theta = (np.arange(polar_total) + 0.5) * (math.pi / polar_total)
    band = (np.cos(edge[:-1]) - np.cos(edge[1:])) * (2.0 * math.pi / azim_total)
    x = np.cos(theta)
    mean = np.zeros(polar_total)
    prev, older = np.ones_like(x), np.zeros_like(x)
    for l in range(DEGREES):
        mean[l] = azim_total * np.sum(band * prev)
        n = l + 1
        a = math.sqrt((4 * n * n - 1) / (n * n))
        b = math.sqrt(l * l / max(4 * l * l - 1, 1))
        prev, older = a * (x * prev - b * older), prev
    return jnp.asarray(np.stack([x, np.sin(theta), band, mean]).astype(np.float32))


def owner_of(sizes):
    row, ta, pa = (lax.axis_index(a) for a in AXES)
    return (row * sizes[1] + ta) * sizes[2] + pa


def stage_kernel(source, target):
    target[...] = source[...]


def pack_kernel(rho, far, shell_out, ends_out):
    rows, polar, azim = rho.shape
    ta, pa = lax.axis_index("ta"), lax.axis_index("pa")
    edge = pa * (rows - 1)
    low = ta % 2 == pa
    for k, half in enumerate((rho, far)):
        at = pl.ds(k * azim, azim)
        shell_out[:, at] = half[edge]
        for r in range(rows):
            ends_out[r : r + 1, at] = jnp.where(low, half[r, polar - 1 : polar, :], half[r, 0:1, :])


def stencil_kernel(
    sizes, rho, far, kappa, far_kappa, shell, mine, theirs, w_high, w_low, keep, send, spec, cells
):
    rows, polar, azim = rho.shape
    half = rows // 2
    row, ta, pa = (lax.axis_index(a) for a in AXES)
    low = ta % 2 == pa
    sub = lax.broadcasted_iota(jnp.int32, (polar, 2 * azim), 0)
    both = lambda a, b: jnp.concatenate([a, b], axis=1)
    at = lambda i: both(rho[i], far[i])
    turned = lambda x: both(x[:, azim:], x[:, :azim])
    outer = turned(shell[...])
    for r in range(half):
        i = pa * half + r
        c = at(i)
        if r == 0:
            ghost = jnp.where(row == 0, c, outer)
            down = jnp.where(pa == 0, ghost, at(jnp.maximum(i - 1, 0)))
        else:
            down = at(i - 1)
        if r == half - 1:
            ghost = jnp.where(row == sizes[0] - 1, c, outer)
            up = jnp.where(pa == 0, at(jnp.minimum(i + 1, rows - 1)), ghost)
        else:
            up = at(i + 1)
        near, other = mine[pl.ds(i, 1), :], turned(theirs[pl.ds(i, 1), :])
        north = jnp.where(ta == 0, turned(c[0:1, :]), jnp.where(low, other, near))
        south = jnp.where(low, near, other)
        south = jnp.where(ta == sizes[1] - 1, turned(c[polar - 1 :, :]), south)
        pol_up = jnp.where(sub == 0, north, pltpu.roll(c, 1, 0))
        pol_down = jnp.where(sub == polar - 1, south, pltpu.roll(c, polar - 1, 0))
        west = pltpu.roll(c, 1, 1)
        east = pltpu.roll(c, 2 * azim - 1, 1)
        lap = up + down + pol_up + pol_down + west + east - 6.0 * c
        new = c + both(kappa[i], far_kappa[i]) * lap
        keep[r] = new[:, :azim]
        send[r] = new[:, azim:]
        cells[r * polar : (r + 1) * polar, :] = new - 1.0
    total = None
    for k, place in enumerate((pa, 1 - pa)):
        at = pl.ds(pl.multiple_of(place * azim, azim), azim)
        term = dot3((w_high[:, at], w_low[:, at]), split(cells[:, k * azim : (k + 1) * azim]), NT)
        total = term if total is None else total + term
    spec[...] = total


def join_kernel(keep, back, out):
    half = keep.shape[0]
    pa = lax.axis_index("pa")
    out[pl.ds(pa * half, half)] = keep[...]
    out[pl.ds((1 - pa) * half, half)] = back[...]


def table_kernel(sizes, coef_ref, trig_ref, high_ref, low_ref, extra_ref, spread_ref, work):
    per, degrees, north = work.shape
    extra_ref[...] = trig_ref[2:4, :]
    start = owner_of(sizes) * per
    lanes = 128
    near = pltpu.roll(coef_ref[: 2 * degrees, :], lanes - start, 1)
    for q in range(per):
        spread_ref[q] = jnp.broadcast_to(near[:, q : q + 1], (2 * degrees, lanes))
    parts = north // lanes
    cut = lambda row, k: jnp.broadcast_to(trig_ref[row : row + 1, k * lanes : (k + 1) * lanes], (8, lanes))
    cos_t = [cut(0, k) for k in range(parts)]
    sin_t = [cut(1, k) for k in range(parts)]
    sub = lax.broadcasted_iota(jnp.int32, (8, lanes), 0)

    def block(step, carry):
        sect, prev, older = carry
        base = pl.multiple_of(step * 8, 8)
        tiles = [[jnp.zeros((8, lanes), F32)] * parts for _ in range(per)]
        for inner in range(8):
            l = base + inner
            factor = coef_ref[pl.ds(2 * degrees + l, 8, stride=0), :]
            grown = [s * (factor * sin_t[k]) for k, s in enumerate(sect)]
            if inner == 0:
                grown = [jnp.where(step == 0, s, g) for s, g in zip(sect, grown)]
            sect = grown
            fresh = []
            for q in range(per):
                a = spread_ref[q, pl.ds(l, 8, stride=0), :]
                ab = spread_ref[q, pl.ds(degrees + l, 8, stride=0), :]
                seed = l == start + q
                line = []
                for k in range(parts):
                    rest = jnp.where(seed, sect[k], 0.0) - ab * older[q][k]
                    new = (a * cos_t[k]) * prev[q][k] + rest
                    tiles[q][k] = jnp.where(sub == inner, new, tiles[q][k])
                    line.append(new)
                fresh.append(line)
            prev, older = fresh, prev
        for q in range(per):
            for k in range(parts):
                work[q, pl.ds(base, 8), k * lanes : (k + 1) * lanes] = tiles[q][k]
        return sect, prev, older

    zero = [[jnp.zeros((8, lanes), F32)] * parts for _ in range(per)]
    lax.fori_loop(0, degrees // 8, block, ([jnp.ones((8, lanes), F32)] * parts, zero, zero))
    square = lambda d: lax.broadcasted_iota(jnp.int32, (north, north), d)
    mirror = jnp.where(square(0) + square(1) == north - 1, 1.0, 0.0).astype(BF16)
    row = lax.broadcasted_iota(jnp.int32, (8, north), 0)
    for q in range(per):
        even = ((row + (start + q)) & 1) == 0
        sign = jnp.concatenate([jnp.where(even, 1.0, -1.0)] * (degrees // 8), axis=0)
        at = pl.ds(q * degrees, degrees)
        for piece, ref in zip(split(work[q]), (high_ref, low_ref)):
            ref[at, :north] = piece
            flipped = lax.dot_general(piece, mirror, NN, preferred_element_type=F32)
            ref[at, north:] = (sign * flipped).astype(BF16)


def solve_kernel(sizes, rows, polar, spec_ref, high_ref, low_ref, extra_ref, out_ref, work_ref):
    n_row, n_ta, n_pa = sizes
    shells = rows * n_row
    pair = spec_ref.shape[1]
    per = pair // 2
    degrees = high_ref.shape[0] // per
    half = rows // n_pa
    band = extra_ref[0:1, :]
    for g in range(n_row):
        for h in range(n_pa):
            parts = [spec_ref[(g * n_ta + t) * n_pa + h] for t in range(n_ta)]
            for r in range(half):
                piece = jnp.concatenate([x[:, r * polar : (r + 1) * polar] for x in parts], axis=1)
                work_ref[pl.ds((g * rows + h * half + r) * pair, pair), :] = piece * band
    table = high_ref[...], low_ref[...]
    wide = dot3(split(work_ref[...]), table, NT)
    slot = lax.broadcasted_iota(jnp.int32, (shells * pair, degrees), 0) & (per - 1)
    picked = wide[:, :degrees]
    for q in range(1, per):
        picked = jnp.where(slot == q, wide[:, q * degrees : (q + 1) * degrees], picked)
    log_eight = math.log(8.0)
    step = log_eight / shells
    degree = lax.broadcasted_iota(jnp.int32, (pair, degrees), 1).astype(F32)
    decay_in = jnp.exp(-step * degree)
    decay_out = jnp.exp(-step * (degree + 1.0))
    scale = jnp.where(degree > 0.0, -1.0 / (4.0 * math.pi * (2.0 * degree + 1.0)), 0.0)
    edges = np.exp(log_eight * (np.arange(shells + 1) / shells - 1.0))
    volume = (edges[1:] ** 3 - edges[:-1] ** 3) / 3.0
    radii = np.exp(log_eight * ((np.arange(shells) + 0.5) / shells - 1.0))
    sub = lax.broadcasted_iota(jnp.int32, (pair, degrees), 0)
    mean = jnp.where((sub == 0) & (owner_of(sizes) == 0), extra_ref[1:2, :degrees], 0.0)
    picked = [picked[i * pair : (i + 1) * pair] + mean for i in range(shells)]
    moments = [picked[i] * float(volume[i]) for i in range(shells)]
    sums = []
    carry = jnp.zeros((pair, degrees), F32)
    for i in range(shells):
        carry = carry * decay_in + moments[i]
        sums.append(carry)
    carry = jnp.zeros((pair, degrees), F32)
    for i in reversed(range(shells)):
        sums[i] = (sums[i] + carry) * (scale * float(1.0 / radii[i]))
        carry = (carry + moments[i]) * decay_out
    coeffs = jnp.concatenate(sums, axis=0)
    spread = jnp.concatenate([jnp.where(slot == q, coeffs, 0.0) for q in range(per)], axis=1)
    field = dot3(split(spread), table, NN)
    for g in range(n_row):
        for h in range(n_pa):
            for t in range(n_ta):
                pieces = []
                for r in range(half):
                    i = g * rows + h * half + r
                    pieces.append(field[i * pair : (i + 1) * pair, t * polar : (t + 1) * polar])
                out_ref[(g * n_ta + t) * n_pa + h] = jnp.concatenate(pieces, axis=1)


def potential_kernel(spec, far, w_high, w_low, out):
    rows, polar, azim = out.shape
    half = rows // 2
    pa = lax.axis_index("pa")
    at = pl.ds(pl.multiple_of(pa * azim, azim), azim)
    table = w_high[:, at], w_low[:, at]
    for part, place in ((spec, pa), (far, 1 - pa)):
        flat = dot3(split(part[...]), table, TN)
        out[pl.ds(place * half, half)] = flat.reshape(half, polar, azim)


def call(kernel, outs, specs, scratch=(), flops=0):
    shapes = tuple(jax.ShapeDtypeStruct(s, d) for s, d in outs)
    return pl.pallas_call(
        kernel,
        out_shape=shapes,
        in_specs=specs,
        out_specs=(VMEM,) * len(outs),
        scratch_shapes=list(scratch),
        compiler_params=PARAMS,
        cost_estimate=pl.CostEstimate(flops=flops, bytes_accessed=2**20, transcendentals=0),
    )


def pair_swap(value, axes, count, first):
    pairs = []
    for i in range(first, count - 1, 2):
        pairs += [(i, i + 1), (i + 1, i)]
    return lax.ppermute(value, axes, pairs)


def halo_pairs(sizes, partner, spare):
    _, n_ta, n_pa = sizes
    number = lambda place: (place[0] * n_ta + place[1]) * n_pa + place[2]
    inside = lambda place: all(0 <= x < n for x, n in zip(place, sizes))
    pairs = []
    for place in np.ndindex(*sizes):
        other = partner(*place)
        if not inside(other):
            other = spare(*place)
        if inside(other):
            pairs.append((number(place), number(other)))
    return pairs


def radial_partner(row, ta, pa):
    return (row + 1, ta, 0) if pa == 1 else (row - 1, ta, 1)


def polar_partner(row, ta, pa):
    return (row, ta + 1 if ta % 2 == pa else ta - 1, pa)


def shards(sizes, density, kappa):
    n_row, n_ta, n_pa = sizes
    rows, polar, azim = density.shape
    owners = n_row * n_ta * n_pa
    per = DEGREES // owners
    polar_total, azim_total = polar * n_ta, azim * n_pa
    half = rows // n_pa
    cells = half * polar
    swap = functools.partial(pair_swap, axes="pa", count=n_pa, first=0)

    far, far_kappa = swap(density), swap(kappa)
    (density,) = call(stage_kernel, ((density.shape, F32),), [VMEM])(density)
    (kappa,) = call(stage_kernel, ((kappa.shape, F32),), [VMEM])(kappa)
    shell, ends = call(
        pack_kernel, (((polar, azim_total), F32), ((rows, azim_total), F32)), [VMEM] * 2
    )(density, far)
    pairs = halo_pairs(sizes, polar_partner, lambda row, ta, pa: (row ^ 1, ta, pa))
    mine = lax.ppermute(ends, AXES, pairs)
    pairs = halo_pairs(sizes, radial_partner, lambda row, ta, pa: (row, ta ^ 1, pa))
    shell = lax.ppermute(shell, AXES, pairs)
    theirs = swap(mine)

    small = small_table(polar_total, azim_total)
    high, low, extra = call(
        functools.partial(table_kernel, sizes),
        (((per * DEGREES, polar_total), BF16),) * 2 + (((2, polar_total), F32),),
        [VMEM] * 2,
        [pltpu.VMEM((per, 2 * DEGREES, 128), F32), pltpu.VMEM((per, DEGREES, polar_total // 2), F32)],
        flops=10**7,
    )(recursion_table(), small)

    waves = wave_table(azim_total, owners)
    keep, send, spec = call(
        functools.partial(stencil_kernel, sizes),
        (((half, polar, azim), F32), ((half, polar, azim), F32), ((2 * DEGREES, cells), F32)),
        [VMEM] * 9,
        [pltpu.VMEM((cells, azim_total), F32)],
    )(density, far, kappa, far_kappa, shell, mine, theirs, *waves)

    back = swap(send)
    spread = functools.partial(
        lax.all_to_all, axis_name=AXES, split_axis=0, concat_axis=0, tiled=True
    )
    spec = spread(spec.reshape(owners, 2 * per, cells))

    (spec,) = call(
        functools.partial(solve_kernel, sizes, rows, polar),
        ((spec.shape, F32),),
        [VMEM] * 4,
        [pltpu.VMEM((rows * n_row * 2 * per, polar_total), F32)],
    )(spec, high, low, extra)
    spec = spread(spec).reshape(2 * DEGREES, cells)
    far = swap(spec)
    (updated,) = call(join_kernel, ((density.shape, F32),), [VMEM] * 2)(keep, back)
    (potential,) = call(potential_kernel, ((density.shape, F32),), [VMEM] * 4)(spec, far, *waves)
    return (updated, potential)


def solution(mesh):
    sizes = tuple(mesh.shape[a] for a in AXES)
    placed = (P(*AXES), P(*AXES))

    def body(density, kappa):
        return shards(sizes, density, kappa)

    return jax.shard_map(body, mesh=mesh, in_specs=placed, out_specs=placed, check_vma=False)
```

```python
import functools
import math

import jax
import jax.numpy as jnp
import numpy as np
from jax import lax
from jax.experimental import pallas as pl
from jax.experimental.pallas import tpu as pltpu
from jax.sharding import PartitionSpec as P


DEGREES = 128
AXES = ("row", "ta", "pa")
VMEM = pl.BlockSpec(memory_space=pltpu.VMEM)
PARAMS = pltpu.CompilerParams(vmem_limit_bytes=16 * 2**20)
F32 = jnp.float32
BF16 = jnp.bfloat16
NT = (((1,), (1,)), ((), ()))
NN = (((1,), (0,)), ((), ()))
TN = (((0,), (0,)), ((), ()))


def split(x):
    high = x.astype(BF16)
    return high, (x - high.astype(F32)).astype(BF16)


def dot3(a, b, dims):
    one = functools.partial(lax.dot_general, dimension_numbers=dims, preferred_element_type=F32)
    axis = 1 - dims[0][0][0]
    rows = a[0].shape[axis]
    wide = one(jnp.concatenate(a, axis=axis), b[0])
    return wide[:rows] + (wide[rows:] + one(a[0], b[1]))


def wave_table(azim_total, owners):
    modes = np.arange(DEGREES).reshape(owners, 1, -1, 1)
    phi = (np.arange(azim_total) + 0.5) * (2.0 * math.pi / azim_total)
    both = np.concatenate([np.cos(modes * phi), np.sin(modes * phi)], axis=1)
    table = both.reshape(2 * DEGREES, azim_total)
    high = table.astype(BF16)
    low = (table - high.astype(np.float64)).astype(BF16)
    return jnp.asarray(high), jnp.asarray(low)


def recursion_table():
    l = np.arange(DEGREES, dtype=np.float64)[:, None]
    m = np.arange(DEGREES, dtype=np.float64)[None, :]
    below = m < l
    a = np.sqrt((4 * l * l - 1) / np.where(below, l * l - m * m, 1.0) * below)
    low = l - 1
    b = np.sqrt(np.maximum(low * low - m * m, 0) / np.maximum(4 * low * low - 1, 1.0))
    sect = np.where(l == 1, math.sqrt(3.0), np.sqrt((2 * l + 1) / np.maximum(2 * l, 1.0)))
    wide = np.broadcast_to(sect, (DEGREES, 128))
    return jnp.asarray(np.concatenate([a, a * b, wide]).astype(np.float32))


def small_table(polar_total, azim_total):
    edge = np.arange(polar_total + 1) * (math.pi / polar_total)
    theta = (np.arange(polar_total) + 0.5) * (math.pi / polar_total)
    band = (np.cos(edge[:-1]) - np.cos(edge[1:])) * (2.0 * math.pi / azim_total)
    x = np.cos(theta)
    mean = np.zeros(polar_total)
    prev, older = np.ones_like(x), np.zeros_like(x)
    for l in range(DEGREES):
        mean[l] = azim_total * np.sum(band * prev)
        n = l + 1
        a = math.sqrt((4 * n * n - 1) / (n * n))
        b = math.sqrt(l * l / max(4 * l * l - 1, 1))
        prev, older = a * (x * prev - b * older), prev
    return jnp.asarray(np.stack([x, np.sin(theta), band, mean]).astype(np.float32))


def owner_of(sizes):
    row, ta, pa = (lax.axis_index(a) for a in AXES)
    return (row * sizes[1] + ta) * sizes[2] + pa


def stage_kernel(source, target):
    target[...] = source[...]


def pack_kernel(rho, far, shell_out, even_out, odd_out):
    rows, polar, azim = rho.shape
    half = rows // 2
    ta, pa = lax.axis_index("ta"), lax.axis_index("pa")
    edge = pa * (rows - 1)
    even = ta % 2 == 0
    for k, part in enumerate((rho, far)):
        at = pl.ds(k * azim, azim)
        shell_out[:, at] = part[edge]
        for r in range(half):
            i = pa * half + r
            first, last = part[i, 0:1, :], part[i, polar - 1 : polar, :]
            even_out[r : r + 1, at] = jnp.where(even, last, first)
            odd_out[r : r + 1, at] = jnp.where(even, first, last)


def stencil_kernel(
    sizes, rho, far, kappa, far_kappa, shell, even_in, odd_in, w_high, w_low, keep, send, spec, cells
):
    rows, polar, azim = rho.shape
    half = rows // 2
    row, ta, pa = (lax.axis_index(a) for a in AXES)
    even = ta % 2 == 0
    sub = lax.broadcasted_iota(jnp.int32, (polar, 2 * azim), 0)
    both = lambda a, b: jnp.concatenate([a, b], axis=1)
    at = lambda i: both(rho[i], far[i])
    turned = lambda x: both(x[:, azim:], x[:, :azim])
    outer = turned(shell[...])
    for r in range(half):
        i = pa * half + r
        c = at(i)
        if r == 0:
            ghost = jnp.where(row == 0, c, outer)
            down = jnp.where(pa == 0, ghost, at(jnp.maximum(i - 1, 0)))
        else:
            down = at(i - 1)
        if r == half - 1:
            ghost = jnp.where(row == sizes[0] - 1, c, outer)
            up = jnp.where(pa == 0, at(jnp.minimum(i + 1, rows - 1)), ghost)
        else:
            up = at(i + 1)
        one, two = even_in[r : r + 1, :], odd_in[r : r + 1, :]
        north = jnp.where(ta == 0, turned(c[0:1, :]), jnp.where(even, two, one))
        south = jnp.where(even, one, two)
        south = jnp.where(ta == sizes[1] - 1, turned(c[polar - 1 :, :]), south)
        pol_up = jnp.where(sub == 0, north, pltpu.roll(c, 1, 0))
        pol_down = jnp.where(sub == polar - 1, south, pltpu.roll(c, polar - 1, 0))
        west = pltpu.roll(c, 1, 1)
        east = pltpu.roll(c, 2 * azim - 1, 1)
        lap = up + down + pol_up + pol_down + west + east - 6.0 * c
        new = c + both(kappa[i], far_kappa[i]) * lap
        keep[r] = new[:, :azim]
        send[r] = new[:, azim:]
        cells[r * polar : (r + 1) * polar, :] = new - 1.0
    total = None
    for k, place in enumerate((pa, 1 - pa)):
        at = pl.ds(pl.multiple_of(place * azim, azim), azim)
        term = dot3((w_high[:, at], w_low[:, at]), split(cells[:, k * azim : (k + 1) * azim]), NT)
        total = term if total is None else total + term
    spec[...] = total


def join_kernel(keep, back, out):
    half = keep.shape[0]
    pa = lax.axis_index("pa")
    out[pl.ds(pa * half, half)] = keep[...]
    out[pl.ds((1 - pa) * half, half)] = back[...]


def table_kernel(sizes, coef_ref, trig_ref, high_ref, low_ref, extra_ref, spread_ref, work):
    per, degrees, north = work.shape
    extra_ref[...] = trig_ref[2:4, :]
    start = owner_of(sizes) * per
    lanes = 128
    near = pltpu.roll(coef_ref[: 2 * degrees, :], lanes - start, 1)
    for q in range(per):
        spread_ref[q] = jnp.broadcast_to(near[:, q : q + 1], (2 * degrees, lanes))
    parts = north // lanes
    cut = lambda row, k: jnp.broadcast_to(trig_ref[row : row + 1, k * lanes : (k + 1) * lanes], (8, lanes))
    cos_t = [cut(0, k) for k in range(parts)]
    sin_t = [cut(1, k) for k in range(parts)]
    sub = lax.broadcasted_iota(jnp.int32, (8, lanes), 0)

    def block(step, carry):
        sect, prev, older = carry
        base = pl.multiple_of(step * 8, 8)
        tiles = [[jnp.zeros((8, lanes), F32)] * parts for _ in range(per)]
        for inner in range(8):
            l = base + inner
            factor = coef_ref[pl.ds(2 * degrees + l, 8, stride=0), :]
            grown = [s * (factor * sin_t[k]) for k, s in enumerate(sect)]
            if inner == 0:
                grown = [jnp.where(step == 0, s, g) for s, g in zip(sect, grown)]
            sect = grown
            fresh = []
            for q in range(per):
                a = spread_ref[q, pl.ds(l, 8, stride=0), :]
                ab = spread_ref[q, pl.ds(degrees + l, 8, stride=0), :]
                seed = l == start + q
                line = []
                for k in range(parts):
                    rest = jnp.where(seed, sect[k], 0.0) - ab * older[q][k]
                    new = (a * cos_t[k]) * prev[q][k] + rest
                    tiles[q][k] = jnp.where(sub == inner, new, tiles[q][k])
                    line.append(new)
                fresh.append(line)
            prev, older = fresh, prev
        for q in range(per):
            for k in range(parts):
                work[q, pl.ds(base, 8), k * lanes : (k + 1) * lanes] = tiles[q][k]
        return sect, prev, older

    zero = [[jnp.zeros((8, lanes), F32)] * parts for _ in range(per)]
    lax.fori_loop(0, degrees // 8, block, ([jnp.ones((8, lanes), F32)] * parts, zero, zero))
    square = lambda d: lax.broadcasted_iota(jnp.int32, (north, north), d)
    mirror = jnp.where(square(0) + square(1) == north - 1, 1.0, 0.0).astype(BF16)
    row = lax.broadcasted_iota(jnp.int32, (8, north), 0)
    for q in range(per):
        even = ((row + (start + q)) & 1) == 0
        sign = jnp.concatenate([jnp.where(even, 1.0, -1.0)] * (degrees // 8), axis=0)
        at = pl.ds(q * degrees, degrees)
        for piece, ref in zip(split(work[q]), (high_ref, low_ref)):
            ref[at, :north] = piece
            flipped = lax.dot_general(piece, mirror, NN, preferred_element_type=F32)
            ref[at, north:] = (sign * flipped).astype(BF16)


def solve_kernel(sizes, rows, polar, spec_ref, high_ref, low_ref, extra_ref, out_ref, work_ref):
    n_row, n_ta, n_pa = sizes
    shells = rows * n_row
    pair = spec_ref.shape[1]
    per = pair // 2
    degrees = high_ref.shape[0] // per
    half = rows // n_pa
    band = extra_ref[0:1, :]
    for g in range(n_row):
        for h in range(n_pa):
            parts = [spec_ref[(g * n_ta + t) * n_pa + h] for t in range(n_ta)]
            for r in range(half):
                piece = jnp.concatenate([x[:, r * polar : (r + 1) * polar] for x in parts], axis=1)
                work_ref[pl.ds((g * rows + h * half + r) * pair, pair), :] = piece * band
    table = high_ref[...], low_ref[...]
    wide = dot3(split(work_ref[...]), table, NT)
    slot = lax.broadcasted_iota(jnp.int32, (shells * pair, degrees), 0) & (per - 1)
    picked = wide[:, :degrees]
    for q in range(1, per):
        picked = jnp.where(slot == q, wide[:, q * degrees : (q + 1) * degrees], picked)
    log_eight = math.log(8.0)
    step = log_eight / shells
    degree = lax.broadcasted_iota(jnp.int32, (pair, degrees), 1).astype(F32)
    decay_in = jnp.exp(-step * degree)
    decay_out = jnp.exp(-step * (degree + 1.0))
    scale = jnp.where(degree > 0.0, -1.0 / (4.0 * math.pi * (2.0 * degree + 1.0)), 0.0)
    edges = np.exp(log_eight * (np.arange(shells + 1) / shells - 1.0))
    volume = (edges[1:] ** 3 - edges[:-1] ** 3) / 3.0
    radii = np.exp(log_eight * ((np.arange(shells) + 0.5) / shells - 1.0))
    sub = lax.broadcasted_iota(jnp.int32, (pair, degrees), 0)
    mean = jnp.where((sub == 0) & (owner_of(sizes) == 0), extra_ref[1:2, :degrees], 0.0)
    picked = [picked[i * pair : (i + 1) * pair] + mean for i in range(shells)]
    moments = [picked[i] * float(volume[i]) for i in range(shells)]
    sums = []
    carry = jnp.zeros((pair, degrees), F32)
    for i in range(shells):
        carry = carry * decay_in + moments[i]
        sums.append(carry)
    carry = jnp.zeros((pair, degrees), F32)
    for i in reversed(range(shells)):
        sums[i] = (sums[i] + carry) * (scale * float(1.0 / radii[i]))
        carry = (carry + moments[i]) * decay_out
    coeffs = jnp.concatenate(sums, axis=0)
    spread = jnp.concatenate([jnp.where(slot == q, coeffs, 0.0) for q in range(per)], axis=1)
    field = dot3(split(spread), table, NN)
    for g in range(n_row):
        for h in range(n_pa):
            for t in range(n_ta):
                pieces = []
                for r in range(half):
                    i = g * rows + h * half + r
                    pieces.append(field[i * pair : (i + 1) * pair, t * polar : (t + 1) * polar])
                out_ref[(g * n_ta + t) * n_pa + h] = jnp.concatenate(pieces, axis=1)


def potential_kernel(spec, far, w_high, w_low, out):
    rows, polar, azim = out.shape
    half = rows // 2
    pa = lax.axis_index("pa")
    at = pl.ds(pl.multiple_of(pa * azim, azim), azim)
    table = w_high[:, at], w_low[:, at]
    for part, place in ((spec, pa), (far, 1 - pa)):
        flat = dot3(split(part[...]), table, TN)
        out[pl.ds(place * half, half)] = flat.reshape(half, polar, azim)


def call(kernel, outs, specs, scratch=(), flops=0):
    shapes = tuple(jax.ShapeDtypeStruct(s, d) for s, d in outs)
    return pl.pallas_call(
        kernel,
        out_shape=shapes,
        in_specs=specs,
        out_specs=(VMEM,) * len(outs),
        scratch_shapes=list(scratch),
        compiler_params=PARAMS,
        cost_estimate=pl.CostEstimate(flops=flops, bytes_accessed=2**20, transcendentals=0),
    )


def pair_swap(value, axes, count, first):
    pairs = []
    for i in range(first, count - 1, 2):
        pairs += [(i, i + 1), (i + 1, i)]
    return lax.ppermute(value, axes, pairs)


def halo_pairs(sizes, partner, spare):
    _, n_ta, n_pa = sizes
    number = lambda place: (place[0] * n_ta + place[1]) * n_pa + place[2]
    inside = lambda place: all(0 <= x < n for x, n in zip(place, sizes))
    pairs = []
    for place in np.ndindex(*sizes):
        other = partner(*place)
        if not inside(other):
            other = spare(*place)
        if inside(other):
            pairs.append((number(place), number(other)))
    return pairs


def radial_partner(row, ta, pa):
    return (row + 1, ta, 0) if pa == 1 else (row - 1, ta, 1)


def polar_partner(first):
    return lambda row, ta, pa: (row, ta + 1 if ta % 2 == first else ta - 1, pa)


def shards(sizes, density, kappa):
    n_row, n_ta, n_pa = sizes
    rows, polar, azim = density.shape
    owners = n_row * n_ta * n_pa
    per = DEGREES // owners
    polar_total, azim_total = polar * n_ta, azim * n_pa
    half = rows // n_pa
    cells = half * polar
    swap = functools.partial(pair_swap, axes="pa", count=n_pa, first=0)

    far, far_kappa = swap(density), swap(kappa)
    (density,) = call(stage_kernel, ((density.shape, F32),), [VMEM])(density)
    (kappa,) = call(stage_kernel, ((kappa.shape, F32),), [VMEM])(kappa)
    ends = ((half, azim_total), F32)
    shell, even, odd = call(
        pack_kernel, (((polar, azim_total), F32), ends, ends), [VMEM] * 2
    )(density, far)
    sides = lambda row, ta, pa: (row, ta ^ 1, pa)
    cores = lambda row, ta, pa: (row, ta, pa ^ 1)
    shell = lax.ppermute(shell, AXES, halo_pairs(sizes, radial_partner, sides))
    even = lax.ppermute(even, AXES, halo_pairs(sizes, polar_partner(0), cores))
    odd = lax.ppermute(odd, AXES, halo_pairs(sizes, polar_partner(1), cores))

    small = small_table(polar_total, azim_total)
    high, low, extra = call(
        functools.partial(table_kernel, sizes),
        (((per * DEGREES, polar_total), BF16),) * 2 + (((2, polar_total), F32),),
        [VMEM] * 2,
        [pltpu.VMEM((per, 2 * DEGREES, 128), F32), pltpu.VMEM((per, DEGREES, polar_total // 2), F32)],
        flops=10**7,
    )(recursion_table(), small)

    waves = wave_table(azim_total, owners)
    keep, send, spec = call(
        functools.partial(stencil_kernel, sizes),
        (((half, polar, azim), F32), ((half, polar, azim), F32), ((2 * DEGREES, cells), F32)),
        [VMEM] * 9,
        [pltpu.VMEM((cells, azim_total), F32)],
    )(density, far, kappa, far_kappa, shell, even, odd, *waves)

    back = swap(send)
    spread = functools.partial(
        lax.all_to_all, axis_name=AXES, split_axis=0, concat_axis=0, tiled=True
    )
    spec = spread(spec.reshape(owners, 2 * per, cells))

    (spec,) = call(
        functools.partial(solve_kernel, sizes, rows, polar),
        ((spec.shape, F32),),
        [VMEM] * 4,
        [pltpu.VMEM((rows * n_row * 2 * per, polar_total), F32)],
    )(spec, high, low, extra)
    spec = spread(spec).reshape(2 * DEGREES, cells)
    far = swap(spec)
    (updated,) = call(join_kernel, ((density.shape, F32),), [VMEM] * 2)(keep, back)
    (potential,) = call(potential_kernel, ((density.shape, F32),), [VMEM] * 4)(spec, far, *waves)
    return (updated, potential)


def solution(mesh):
    sizes = tuple(mesh.shape[a] for a in AXES)
    placed = (P(*AXES), P(*AXES))

    def body(density, kappa):
        return shards(sizes, density, kappa)

    return jax.shard_map(body, mesh=mesh, in_specs=placed, out_specs=placed, check_vma=False)
```

```python
import functools
import math

import jax
import jax.numpy as jnp
import numpy as np
from jax import lax
from jax.experimental import pallas as pl
from jax.experimental.pallas import tpu as pltpu
from jax.sharding import PartitionSpec as P


DEGREES = 128
AXES = ("row", "ta", "pa")
VMEM = pl.BlockSpec(memory_space=pltpu.VMEM)
PARAMS = pltpu.CompilerParams(vmem_limit_bytes=16 * 2**20)
F32 = jnp.float32
BF16 = jnp.bfloat16
NT = (((1,), (1,)), ((), ()))
NN = (((1,), (0,)), ((), ()))
TN = (((0,), (0,)), ((), ()))


def split(x):
    high = x.astype(BF16)
    return high, (x - high.astype(F32)).astype(BF16)


def dot3(a, b, dims):
    one = functools.partial(lax.dot_general, dimension_numbers=dims, preferred_element_type=F32)
    axis = 1 - dims[0][0][0]
    rows = a[0].shape[axis]
    wide = one(jnp.concatenate(a, axis=axis), b[0])
    return wide[:rows] + (wide[rows:] + one(a[0], b[1]))


def wave_table(azim_total, owners):
    modes = np.arange(DEGREES).reshape(owners, 1, -1, 1)
    phi = (np.arange(azim_total) + 0.5) * (2.0 * math.pi / azim_total)
    both = np.concatenate([np.cos(modes * phi), np.sin(modes * phi)], axis=1)
    table = both.reshape(2 * DEGREES, azim_total)
    high = table.astype(BF16)
    low = (table - high.astype(np.float64)).astype(BF16)
    return jnp.asarray(high), jnp.asarray(low)


def recursion_table():
    l = np.arange(DEGREES, dtype=np.float64)[:, None]
    m = np.arange(DEGREES, dtype=np.float64)[None, :]
    below = m < l
    a = np.sqrt((4 * l * l - 1) / np.where(below, l * l - m * m, 1.0) * below)
    low = l - 1
    b = np.sqrt(np.maximum(low * low - m * m, 0) / np.maximum(4 * low * low - 1, 1.0))
    sect = np.where(l == 1, math.sqrt(3.0), np.sqrt((2 * l + 1) / np.maximum(2 * l, 1.0)))
    wide = np.broadcast_to(sect, (DEGREES, 128))
    return jnp.asarray(np.concatenate([a, a * b, wide]).astype(np.float32))


def small_table(polar_total, azim_total):
    edge = np.arange(polar_total + 1) * (math.pi / polar_total)
    theta = (np.arange(polar_total) + 0.5) * (math.pi / polar_total)
    band = (np.cos(edge[:-1]) - np.cos(edge[1:])) * (2.0 * math.pi / azim_total)
    x = np.cos(theta)
    mean = np.zeros(polar_total)
    prev, older = np.ones_like(x), np.zeros_like(x)
    for l in range(DEGREES):
        mean[l] = azim_total * np.sum(band * prev)
        n = l + 1
        a = math.sqrt((4 * n * n - 1) / (n * n))
        b = math.sqrt(l * l / max(4 * l * l - 1, 1))
        prev, older = a * (x * prev - b * older), prev
    return jnp.asarray(np.stack([x, np.sin(theta), band, mean]).astype(np.float32))


def owner_of(sizes):
    row, ta, pa = (lax.axis_index(a) for a in AXES)
    return (row * sizes[1] + ta) * sizes[2] + pa


def stage_kernel(source, target):
    target[...] = source[...]


def pack_kernel(rho, far, shell_out, even_out, odd_out):
    rows, polar, azim = rho.shape
    half = rows // 2
    ta, pa = lax.axis_index("ta"), lax.axis_index("pa")
    edge = pa * (rows - 1)
    even = ta % 2 == 0
    for k, part in enumerate((rho, far)):
        at = pl.ds(k * azim, azim)
        shell_out[:, at] = part[edge]
        for r in range(half):
            i = pa * half + r
            first, last = part[i, 0:1, :], part[i, polar - 1 : polar, :]
            even_out[r : r + 1, at] = jnp.where(even, last, first)
            odd_out[r : r + 1, at] = jnp.where(even, first, last)


def both(a, b):
    return jnp.concatenate([a, b], axis=1)


def early_kernel(sizes, rho, far, kappa, far_kappa, w_high, w_low, base):
    rows, polar, azim = rho.shape
    half = rows // 2
    row, ta, pa = (lax.axis_index(a) for a in AXES)
    sub = lax.broadcasted_iota(jnp.int32, (polar, 2 * azim), 0)
    at = lambda i: both(rho[i], far[i])
    turned = lambda x: both(x[:, azim:], x[:, :azim])
    for r in range(half):
        i = pa * half + r
        c = at(i)
        if r == 0:
            edge = jnp.where(row == 0, c, 0.0)
            down = jnp.where(pa == 0, edge, at(jnp.maximum(i - 1, 0)))
        else:
            down = at(i - 1)
        if r == half - 1:
            edge = jnp.where(row == sizes[0] - 1, c, 0.0)
            up = jnp.where(pa == 0, at(jnp.minimum(i + 1, rows - 1)), edge)
        else:
            up = at(i + 1)
        north = jnp.where(ta == 0, turned(c[0:1, :]), 0.0)
        south = jnp.where(ta == sizes[1] - 1, turned(c[polar - 1 :, :]), 0.0)
        pol_up = jnp.where(sub == 0, north, pltpu.roll(c, 1, 0))
        pol_down = jnp.where(sub == polar - 1, south, pltpu.roll(c, polar - 1, 0))
        west = pltpu.roll(c, 1, 1)
        east = pltpu.roll(c, 2 * azim - 1, 1)
        lap = up + down + pol_up + pol_down + west + east - 6.0 * c
        base[r * polar : (r + 1) * polar, :] = c + both(kappa[i], far_kappa[i]) * lap


def stencil_kernel(
    sizes, base, kappa, far_kappa, shell, even_in, odd_in, w_high, w_low, keep, send, spec, cells
):
    rows, polar, azim = kappa.shape
    half = rows // 2
    row, ta, pa = (lax.axis_index(a) for a in AXES)
    even = ta % 2 == 0
    outer = both(shell[:, azim:], shell[:, :azim])
    for r in range(half):
        i = pa * half + r
        k = both(kappa[i], far_kappa[i])
        new = base[r * polar : (r + 1) * polar, :]
        if r == 0:
            new = new + jnp.where((pa == 0) & (row > 0), k * outer, 0.0)
        if r == half - 1:
            new = new + jnp.where((pa == 1) & (row < sizes[0] - 1), k * outer, 0.0)
        one, two = even_in[r : r + 1, :], odd_in[r : r + 1, :]
        north = jnp.where(ta == 0, 0.0, jnp.where(even, two, one)) * k[0:1, :]
        south = jnp.where(ta == sizes[1] - 1, 0.0, jnp.where(even, one, two)) * k[polar - 1 :, :]
        top, low = new[0:8, :], new[polar - 8 :, :]
        sub = lax.broadcasted_iota(jnp.int32, top.shape, 0)
        top = top + jnp.where(sub == 0, north, 0.0)
        low = low + jnp.where(sub == 7, south, 0.0)
        new = jnp.concatenate([top, new[8 : polar - 8, :], low], axis=0)
        keep[r] = new[:, :azim]
        send[r] = new[:, azim:]
        cells[r * polar : (r + 1) * polar, :] = new - 1.0
    total = None
    for k, place in enumerate((pa, 1 - pa)):
        at = pl.ds(pl.multiple_of(place * azim, azim), azim)
        term = dot3((w_high[:, at], w_low[:, at]), split(cells[:, k * azim : (k + 1) * azim]), NT)
        total = term if total is None else total + term
    spec[...] = total


def join_kernel(keep, back, out):
    half = keep.shape[0]
    pa = lax.axis_index("pa")
    out[pl.ds(pa * half, half)] = keep[...]
    out[pl.ds((1 - pa) * half, half)] = back[...]


def table_kernel(sizes, coef_ref, trig_ref, high_ref, low_ref, extra_ref, spread_ref, work):
    per, degrees, north = work.shape
    extra_ref[...] = trig_ref[2:4, :]
    start = owner_of(sizes) * per
    lanes = 128
    near = pltpu.roll(coef_ref[: 2 * degrees, :], lanes - start, 1)
    for q in range(per):
        spread_ref[q] = jnp.broadcast_to(near[:, q : q + 1], (2 * degrees, lanes))
    parts = north // lanes
    cut = lambda row, k: jnp.broadcast_to(trig_ref[row : row + 1, k * lanes : (k + 1) * lanes], (8, lanes))
    cos_t = [cut(0, k) for k in range(parts)]
    sin_t = [cut(1, k) for k in range(parts)]
    sub = lax.broadcasted_iota(jnp.int32, (8, lanes), 0)

    def block(step, carry):
        sect, prev, older = carry
        base = pl.multiple_of(step * 8, 8)
        tiles = [[jnp.zeros((8, lanes), F32)] * parts for _ in range(per)]
        for inner in range(8):
            l = base + inner
            factor = coef_ref[pl.ds(2 * degrees + l, 8, stride=0), :]
            grown = [s * (factor * sin_t[k]) for k, s in enumerate(sect)]
            if inner == 0:
                grown = [jnp.where(step == 0, s, g) for s, g in zip(sect, grown)]
            sect = grown
            fresh = []
            for q in range(per):
                a = spread_ref[q, pl.ds(l, 8, stride=0), :]
                ab = spread_ref[q, pl.ds(degrees + l, 8, stride=0), :]
                seed = l == start + q
                line = []
                for k in range(parts):
                    rest = jnp.where(seed, sect[k], 0.0) - ab * older[q][k]
                    new = (a * cos_t[k]) * prev[q][k] + rest
                    tiles[q][k] = jnp.where(sub == inner, new, tiles[q][k])
                    line.append(new)
                fresh.append(line)
            prev, older = fresh, prev
        for q in range(per):
            for k in range(parts):
                work[q, pl.ds(base, 8), k * lanes : (k + 1) * lanes] = tiles[q][k]
        return sect, prev, older

    zero = [[jnp.zeros((8, lanes), F32)] * parts for _ in range(per)]
    lax.fori_loop(0, degrees // 8, block, ([jnp.ones((8, lanes), F32)] * parts, zero, zero))
    square = lambda d: lax.broadcasted_iota(jnp.int32, (north, north), d)
    mirror = jnp.where(square(0) + square(1) == north - 1, 1.0, 0.0).astype(BF16)
    row = lax.broadcasted_iota(jnp.int32, (8, north), 0)
    for q in range(per):
        even = ((row + (start + q)) & 1) == 0
        sign = jnp.concatenate([jnp.where(even, 1.0, -1.0)] * (degrees // 8), axis=0)
        at = pl.ds(q * degrees, degrees)
        for piece, ref in zip(split(work[q]), (high_ref, low_ref)):
            ref[at, :north] = piece
            flipped = lax.dot_general(piece, mirror, NN, preferred_element_type=F32)
            ref[at, north:] = (sign * flipped).astype(BF16)


def solve_kernel(sizes, rows, polar, spec_ref, high_ref, low_ref, extra_ref, out_ref, work_ref):
    n_row, n_ta, n_pa = sizes
    shells = rows * n_row
    pair = spec_ref.shape[1]
    per = pair // 2
    degrees = high_ref.shape[0] // per
    half = rows // n_pa
    band = extra_ref[0:1, :]
    for g in range(n_row):
        for h in range(n_pa):
            parts = [spec_ref[(g * n_ta + t) * n_pa + h] for t in range(n_ta)]
            for r in range(half):
                piece = jnp.concatenate([x[:, r * polar : (r + 1) * polar] for x in parts], axis=1)
                work_ref[pl.ds((g * rows + h * half + r) * pair, pair), :] = piece * band
    table = high_ref[...], low_ref[...]
    wide = dot3(split(work_ref[...]), table, NT)
    slot = lax.broadcasted_iota(jnp.int32, (shells * pair, degrees), 0) & (per - 1)
    picked = wide[:, :degrees]
    for q in range(1, per):
        picked = jnp.where(slot == q, wide[:, q * degrees : (q + 1) * degrees], picked)
    log_eight = math.log(8.0)
    step = log_eight / shells
    degree = lax.broadcasted_iota(jnp.int32, (pair, degrees), 1).astype(F32)
    decay_in = jnp.exp(-step * degree)
    decay_out = jnp.exp(-step * (degree + 1.0))
    scale = jnp.where(degree > 0.0, -1.0 / (4.0 * math.pi * (2.0 * degree + 1.0)), 0.0)
    edges = np.exp(log_eight * (np.arange(shells + 1) / shells - 1.0))
    volume = (edges[1:] ** 3 - edges[:-1] ** 3) / 3.0
    radii = np.exp(log_eight * ((np.arange(shells) + 0.5) / shells - 1.0))
    sub = lax.broadcasted_iota(jnp.int32, (pair, degrees), 0)
    mean = jnp.where((sub == 0) & (owner_of(sizes) == 0), extra_ref[1:2, :degrees], 0.0)
    picked = [picked[i * pair : (i + 1) * pair] + mean for i in range(shells)]
    moments = [picked[i] * float(volume[i]) for i in range(shells)]
    sums = []
    carry = jnp.zeros((pair, degrees), F32)
    for i in range(shells):
        carry = carry * decay_in + moments[i]
        sums.append(carry)
    carry = jnp.zeros((pair, degrees), F32)
    for i in reversed(range(shells)):
        sums[i] = (sums[i] + carry) * (scale * float(1.0 / radii[i]))
        carry = (carry + moments[i]) * decay_out
    coeffs = jnp.concatenate(sums, axis=0)
    spread = jnp.concatenate([jnp.where(slot == q, coeffs, 0.0) for q in range(per)], axis=1)
    field = dot3(split(spread), table, NN)
    for g in range(n_row):
        for h in range(n_pa):
            for t in range(n_ta):
                pieces = []
                for r in range(half):
                    i = g * rows + h * half + r
                    pieces.append(field[i * pair : (i + 1) * pair, t * polar : (t + 1) * polar])
                out_ref[(g * n_ta + t) * n_pa + h] = jnp.concatenate(pieces, axis=1)


def potential_kernel(spec, far, w_high, w_low, out):
    rows, polar, azim = out.shape
    half = rows // 2
    pa = lax.axis_index("pa")
    at = pl.ds(pl.multiple_of(pa * azim, azim), azim)
    table = w_high[:, at], w_low[:, at]
    for part, place in ((spec, pa), (far, 1 - pa)):
        flat = dot3(split(part[...]), table, TN)
        out[pl.ds(place * half, half)] = flat.reshape(half, polar, azim)


def call(kernel, outs, specs, scratch=(), flops=0):
    shapes = tuple(jax.ShapeDtypeStruct(s, d) for s, d in outs)
    return pl.pallas_call(
        kernel,
        out_shape=shapes,
        in_specs=specs,
        out_specs=(VMEM,) * len(outs),
        scratch_shapes=list(scratch),
        compiler_params=PARAMS,
        cost_estimate=pl.CostEstimate(flops=flops, bytes_accessed=2**20, transcendentals=0),
    )


def pair_swap(value, axes, count, first):
    pairs = []
    for i in range(first, count - 1, 2):
        pairs += [(i, i + 1), (i + 1, i)]
    return lax.ppermute(value, axes, pairs)


def halo_pairs(sizes, partner, spare):
    _, n_ta, n_pa = sizes
    number = lambda place: (place[0] * n_ta + place[1]) * n_pa + place[2]
    inside = lambda place: all(0 <= x < n for x, n in zip(place, sizes))
    pairs = []
    for place in np.ndindex(*sizes):
        other = partner(*place)
        if not inside(other):
            other = spare(*place)
        if inside(other):
            pairs.append((number(place), number(other)))
    return pairs


def radial_partner(row, ta, pa):
    return (row + 1, ta, 0) if pa == 1 else (row - 1, ta, 1)


def polar_partner(first):
    return lambda row, ta, pa: (row, ta + 1 if ta % 2 == first else ta - 1, pa)


def shards(sizes, density, kappa):
    n_row, n_ta, n_pa = sizes
    rows, polar, azim = density.shape
    owners = n_row * n_ta * n_pa
    per = DEGREES // owners
    polar_total, azim_total = polar * n_ta, azim * n_pa
    half = rows // n_pa
    cells = half * polar
    swap = functools.partial(pair_swap, axes="pa", count=n_pa, first=0)

    far, far_kappa = swap(density), swap(kappa)
    (density,) = call(stage_kernel, ((density.shape, F32),), [VMEM])(density)
    (kappa,) = call(stage_kernel, ((kappa.shape, F32),), [VMEM])(kappa)
    ends = ((half, azim_total), F32)
    shell, even, odd = call(
        pack_kernel, (((polar, azim_total), F32), ends, ends), [VMEM] * 2
    )(density, far)
    sides = lambda row, ta, pa: (row, ta ^ 1, pa)
    cores = lambda row, ta, pa: (row, ta, pa ^ 1)
    shell = lax.ppermute(shell, AXES, halo_pairs(sizes, radial_partner, sides))
    even = lax.ppermute(even, AXES, halo_pairs(sizes, polar_partner(0), cores))
    odd = lax.ppermute(odd, AXES, halo_pairs(sizes, polar_partner(1), cores))

    small = small_table(polar_total, azim_total)
    high, low, extra = call(
        functools.partial(table_kernel, sizes),
        (((per * DEGREES, polar_total), BF16),) * 2 + (((2, polar_total), F32),),
        [VMEM] * 2,
        [pltpu.VMEM((per, 2 * DEGREES, 128), F32), pltpu.VMEM((per, DEGREES, polar_total // 2), F32)],
        flops=10**7,
    )(recursion_table(), small)

    waves = wave_table(azim_total, owners)
    (base,) = call(
        functools.partial(early_kernel, sizes), (((cells, azim_total), F32),), [VMEM] * 6
    )(density, far, kappa, far_kappa, *waves)
    keep, send, spec = call(
        functools.partial(stencil_kernel, sizes),
        (((half, polar, azim), F32), ((half, polar, azim), F32), ((2 * DEGREES, cells), F32)),
        [VMEM] * 8,
        [pltpu.VMEM((cells, azim_total), F32)],
    )(base, kappa, far_kappa, shell, even, odd, *waves)

    back = swap(send)
    spread = functools.partial(
        lax.all_to_all, axis_name=AXES, split_axis=0, concat_axis=0, tiled=True
    )
    spec = spread(spec.reshape(owners, 2 * per, cells))

    (spec,) = call(
        functools.partial(solve_kernel, sizes, rows, polar),
        ((spec.shape, F32),),
        [VMEM] * 4,
        [pltpu.VMEM((rows * n_row * 2 * per, polar_total), F32)],
    )(spec, high, low, extra)
    spec = spread(spec).reshape(2 * DEGREES, cells)
    far = swap(spec)
    (updated,) = call(join_kernel, ((density.shape, F32),), [VMEM] * 2)(keep, back)
    (potential,) = call(potential_kernel, ((density.shape, F32),), [VMEM] * 4)(spec, far, *waves)
    return (updated, potential)


def solution(mesh):
    sizes = tuple(mesh.shape[a] for a in AXES)
    placed = (P(*AXES), P(*AXES))

    def body(density, kappa):
        return shards(sizes, density, kappa)

    return jax.shard_map(body, mesh=mesh, in_specs=placed, out_specs=placed, check_vma=False)
```

```python
import functools
import math

import jax
import jax.numpy as jnp
import numpy as np
from jax import lax
from jax.experimental import pallas as pl
from jax.experimental.pallas import tpu as pltpu
from jax.sharding import PartitionSpec as P


DEGREES = 128
AXES = ("row", "ta", "pa")
VMEM = pl.BlockSpec(memory_space=pltpu.VMEM)
PARAMS = pltpu.CompilerParams(vmem_limit_bytes=16 * 2**20)
F32 = jnp.float32
BF16 = jnp.bfloat16
NT = (((1,), (1,)), ((), ()))
NN = (((1,), (0,)), ((), ()))
TN = (((0,), (0,)), ((), ()))


def split(x):
    high = x.astype(BF16)
    return high, (x - high.astype(F32)).astype(BF16)


def dot3(a, b, dims):
    one = functools.partial(lax.dot_general, dimension_numbers=dims, preferred_element_type=F32)
    axis = 1 - dims[0][0][0]
    rows = a[0].shape[axis]
    wide = one(jnp.concatenate(a, axis=axis), b[0])
    return wide[:rows] + (wide[rows:] + one(a[0], b[1]))


def wave_table(azim_total, owners):
    modes = np.arange(DEGREES).reshape(owners, 1, -1, 1)
    phi = (np.arange(azim_total) + 0.5) * (2.0 * math.pi / azim_total)
    both = np.concatenate([np.cos(modes * phi), np.sin(modes * phi)], axis=1)
    table = both.reshape(2 * DEGREES, azim_total)
    high = table.astype(BF16)
    low = (table - high.astype(np.float64)).astype(BF16)
    return jnp.asarray(high), jnp.asarray(low)


def recursion_table():
    l = np.arange(DEGREES, dtype=np.float64)[:, None]
    m = np.arange(DEGREES, dtype=np.float64)[None, :]
    below = m < l
    a = np.sqrt((4 * l * l - 1) / np.where(below, l * l - m * m, 1.0) * below)
    low = l - 1
    b = np.sqrt(np.maximum(low * low - m * m, 0) / np.maximum(4 * low * low - 1, 1.0))
    sect = np.where(l == 1, math.sqrt(3.0), np.sqrt((2 * l + 1) / np.maximum(2 * l, 1.0)))
    wide = np.broadcast_to(sect, (DEGREES, 128))
    spare = np.zeros((8, 128))
    return jnp.asarray(np.concatenate([a, a * b, wide, spare]).astype(np.float32))


def small_table(polar_total, azim_total):
    edge = np.arange(polar_total + 1) * (math.pi / polar_total)
    theta = (np.arange(polar_total) + 0.5) * (math.pi / polar_total)
    band = (np.cos(edge[:-1]) - np.cos(edge[1:])) * (2.0 * math.pi / azim_total)
    x = np.cos(theta)
    mean = np.zeros(polar_total)
    prev, older = np.ones_like(x), np.zeros_like(x)
    for l in range(DEGREES):
        mean[l] = azim_total * np.sum(band * prev)
        n = l + 1
        a = math.sqrt((4 * n * n - 1) / (n * n))
        b = math.sqrt(l * l / max(4 * l * l - 1, 1))
        prev, older = a * (x * prev - b * older), prev
    return jnp.asarray(np.stack([x, np.sin(theta), band, mean]).astype(np.float32))


def owner_of(sizes):
    row, ta, pa = (lax.axis_index(a) for a in AXES)
    return (row * sizes[1] + ta) * sizes[2] + pa


def stage_kernel(source, target):
    target[...] = source[...]


def pack_kernel(rho, far, shell_out, even_out, odd_out):
    rows, polar, azim = rho.shape
    half = rows // 2
    ta, pa = lax.axis_index("ta"), lax.axis_index("pa")
    edge = pa * (rows - 1)
    even = ta % 2 == 0
    for k, part in enumerate((rho, far)):
        at = pl.ds(k * azim, azim)
        shell_out[:, at] = part[edge]
        for r in range(half):
            i = pa * half + r
            first, last = part[i, 0:1, :], part[i, polar - 1 : polar, :]
            even_out[r : r + 1, at] = jnp.where(even, last, first)
            odd_out[r : r + 1, at] = jnp.where(even, first, last)


def both(a, b):
    return jnp.concatenate([a, b], axis=1)


def early_kernel(sizes, rho, far, kappa, far_kappa, w_high, w_low, base):
    rows, polar, azim = rho.shape
    half = rows // 2
    row, ta, pa = (lax.axis_index(a) for a in AXES)
    sub = lax.broadcasted_iota(jnp.int32, (polar, 2 * azim), 0)
    at = lambda i: both(rho[i], far[i])
    turned = lambda x: both(x[:, azim:], x[:, :azim])
    for r in range(half):
        i = pa * half + r
        c = at(i)
        if r == 0:
            edge = jnp.where(row == 0, c, 0.0)
            down = jnp.where(pa == 0, edge, at(jnp.maximum(i - 1, 0)))
        else:
            down = at(i - 1)
        if r == half - 1:
            edge = jnp.where(row == sizes[0] - 1, c, 0.0)
            up = jnp.where(pa == 0, at(jnp.minimum(i + 1, rows - 1)), edge)
        else:
            up = at(i + 1)
        north = jnp.where(ta == 0, turned(c[0:1, :]), 0.0)
        south = jnp.where(ta == sizes[1] - 1, turned(c[polar - 1 :, :]), 0.0)
        pol_up = jnp.where(sub == 0, north, pltpu.roll(c, 1, 0))
        pol_down = jnp.where(sub == polar - 1, south, pltpu.roll(c, polar - 1, 0))
        west = pltpu.roll(c, 1, 1)
        east = pltpu.roll(c, 2 * azim - 1, 1)
        lap = up + down + pol_up + pol_down + west + east - 6.0 * c
        base[r * polar : (r + 1) * polar, :] = c + both(kappa[i], far_kappa[i]) * lap


def stencil_kernel(
    sizes, base, kappa, far_kappa, shell, even_in, odd_in, w_high, w_low, keep, send, spec, cells
):
    rows, polar, azim = kappa.shape
    half = rows // 2
    row, ta, pa = (lax.axis_index(a) for a in AXES)
    even = ta % 2 == 0
    outer = both(shell[:, azim:], shell[:, :azim])
    for r in range(half):
        i = pa * half + r
        k = both(kappa[i], far_kappa[i])
        new = base[r * polar : (r + 1) * polar, :]
        if r == 0:
            new = new + jnp.where((pa == 0) & (row > 0), k * outer, 0.0)
        if r == half - 1:
            new = new + jnp.where((pa == 1) & (row < sizes[0] - 1), k * outer, 0.0)
        one, two = even_in[r : r + 1, :], odd_in[r : r + 1, :]
        north = jnp.where(ta == 0, 0.0, jnp.where(even, two, one)) * k[0:1, :]
        south = jnp.where(ta == sizes[1] - 1, 0.0, jnp.where(even, one, two)) * k[polar - 1 :, :]
        top, low = new[0:8, :], new[polar - 8 :, :]
        sub = lax.broadcasted_iota(jnp.int32, top.shape, 0)
        top = top + jnp.where(sub == 0, north, 0.0)
        low = low + jnp.where(sub == 7, south, 0.0)
        new = jnp.concatenate([top, new[8 : polar - 8, :], low], axis=0)
        keep[r] = new[:, :azim]
        send[r] = new[:, azim:]
        cells[r * polar : (r + 1) * polar, :] = new - 1.0
    total = None
    for k, place in enumerate((pa, 1 - pa)):
        at = pl.ds(pl.multiple_of(place * azim, azim), azim)
        term = dot3((w_high[:, at], w_low[:, at]), split(cells[:, k * azim : (k + 1) * azim]), NT)
        total = term if total is None else total + term
    spec[...] = total


def join_kernel(keep, back, out):
    half = keep.shape[0]
    pa = lax.axis_index("pa")
    out[pl.ds(pa * half, half)] = keep[...]
    out[pl.ds((1 - pa) * half, half)] = back[...]


def table_kernel(sizes, coef_ref, trig_ref, high_ref, low_ref, extra_ref, spread_ref, work):
    per, degrees, north = work.shape
    extra_ref[...] = trig_ref[2:4, :]
    start = owner_of(sizes) * per
    lanes = 128
    near = pltpu.roll(coef_ref[: 2 * degrees, :], lanes - start, 1)
    for q in range(per):
        spread_ref[q, : 2 * degrees, :] = jnp.broadcast_to(near[:, q : q + 1], (2 * degrees, lanes))
    parts = north // lanes
    cut = lambda row, k: jnp.broadcast_to(trig_ref[row : row + 1, k * lanes : (k + 1) * lanes], (8, lanes))
    cos_t = [cut(0, k) for k in range(parts)]
    sin_t = [cut(1, k) for k in range(parts)]
    sub = lax.broadcasted_iota(jnp.int32, (8, lanes), 0)

    def block(step, carry):
        sect, prev, older = carry
        base = pl.multiple_of(step * 8, 8)
        tiles = [[jnp.zeros((8, lanes), F32)] * parts for _ in range(per)]
        for inner in range(8):
            l = base + inner
            factor = coef_ref[pl.ds(2 * degrees + l, 8, stride=0), :]
            grown = [s * (factor * sin_t[k]) for k, s in enumerate(sect)]
            if inner == 0:
                grown = [jnp.where(step == 0, s, g) for s, g in zip(sect, grown)]
            sect = grown
            fresh = []
            for q in range(per):
                a = spread_ref[q, pl.ds(l, 8, stride=0), :]
                ab = spread_ref[q, pl.ds(degrees + l, 8, stride=0), :]
                seed = l == start + q
                line = []
                for k in range(parts):
                    rest = jnp.where(seed, sect[k], 0.0) - ab * older[q][k]
                    new = (a * cos_t[k]) * prev[q][k] + rest
                    tiles[q][k] = jnp.where(sub == inner, new, tiles[q][k])
                    line.append(new)
                fresh.append(line)
            prev, older = fresh, prev
        for q in range(per):
            for k in range(parts):
                work[q, pl.ds(base, 8), k * lanes : (k + 1) * lanes] = tiles[q][k]
        return sect, prev, older

    zero = [[jnp.zeros((8, lanes), F32)] * parts for _ in range(per)]
    lax.fori_loop(0, degrees // 8, block, ([jnp.ones((8, lanes), F32)] * parts, zero, zero))
    square = lambda d: lax.broadcasted_iota(jnp.int32, (north, north), d)
    mirror = jnp.where(square(0) + square(1) == north - 1, 1.0, 0.0).astype(BF16)
    row = lax.broadcasted_iota(jnp.int32, (8, north), 0)
    for q in range(per):
        even = ((row + (start + q)) & 1) == 0
        sign = jnp.concatenate([jnp.where(even, 1.0, -1.0)] * (degrees // 8), axis=0)
        at = pl.ds(q * degrees, degrees)
        for piece, ref in zip(split(work[q]), (high_ref, low_ref)):
            ref[at, :north] = piece
            flipped = lax.dot_general(piece, mirror, NN, preferred_element_type=F32)
            ref[at, north:] = (sign * flipped).astype(BF16)


def solve_kernel(sizes, rows, polar, spec_ref, high_ref, low_ref, extra_ref, out_ref, work_ref):
    n_row, n_ta, n_pa = sizes
    shells = rows * n_row
    pair = spec_ref.shape[1]
    per = pair // 2
    degrees = high_ref.shape[0] // per
    half = rows // n_pa
    band = extra_ref[0:1, :]
    for g in range(n_row):
        for h in range(n_pa):
            parts = [spec_ref[(g * n_ta + t) * n_pa + h] for t in range(n_ta)]
            for r in range(half):
                piece = jnp.concatenate([x[:, r * polar : (r + 1) * polar] for x in parts], axis=1)
                work_ref[pl.ds((g * rows + h * half + r) * pair, pair), :] = piece * band
    table = high_ref[...], low_ref[...]
    wide = dot3(split(work_ref[...]), table, NT)
    slot = lax.broadcasted_iota(jnp.int32, (shells * pair, degrees), 0) & (per - 1)
    picked = wide[:, :degrees]
    for q in range(1, per):
        picked = jnp.where(slot == q, wide[:, q * degrees : (q + 1) * degrees], picked)
    log_eight = math.log(8.0)
    step = log_eight / shells
    degree = lax.broadcasted_iota(jnp.int32, (pair, degrees), 1).astype(F32)
    decay_in = jnp.exp(-step * degree)
    decay_out = jnp.exp(-step * (degree + 1.0))
    scale = jnp.where(degree > 0.0, -1.0 / (4.0 * math.pi * (2.0 * degree + 1.0)), 0.0)
    edges = np.exp(log_eight * (np.arange(shells + 1) / shells - 1.0))
    volume = (edges[1:] ** 3 - edges[:-1] ** 3) / 3.0
    radii = np.exp(log_eight * ((np.arange(shells) + 0.5) / shells - 1.0))
    sub = lax.broadcasted_iota(jnp.int32, (pair, degrees), 0)
    mean = jnp.where((sub == 0) & (owner_of(sizes) == 0), extra_ref[1:2, :degrees], 0.0)
    picked = [picked[i * pair : (i + 1) * pair] + mean for i in range(shells)]
    moments = [picked[i] * float(volume[i]) for i in range(shells)]
    sums = []
    carry = jnp.zeros((pair, degrees), F32)
    for i in range(shells):
        carry = carry * decay_in + moments[i]
        sums.append(carry)
    carry = jnp.zeros((pair, degrees), F32)
    for i in reversed(range(shells)):
        sums[i] = (sums[i] + carry) * (scale * float(1.0 / radii[i]))
        carry = (carry + moments[i]) * decay_out
    coeffs = jnp.concatenate(sums, axis=0)
    spread = jnp.concatenate([jnp.where(slot == q, coeffs, 0.0) for q in range(per)], axis=1)
    field = dot3(split(spread), table, NN)
    for g in range(n_row):
        for h in range(n_pa):
            for t in range(n_ta):
                pieces = []
                for r in range(half):
                    i = g * rows + h * half + r
                    pieces.append(field[i * pair : (i + 1) * pair, t * polar : (t + 1) * polar])
                out_ref[(g * n_ta + t) * n_pa + h] = jnp.concatenate(pieces, axis=1)


def potential_kernel(spec, far, w_high, w_low, out):
    rows, polar, azim = out.shape
    half = rows // 2
    pa = lax.axis_index("pa")
    at = pl.ds(pl.multiple_of(pa * azim, azim), azim)
    table = w_high[:, at], w_low[:, at]
    for part, place in ((spec, pa), (far, 1 - pa)):
        flat = dot3(split(part[...]), table, TN)
        out[pl.ds(place * half, half)] = flat.reshape(half, polar, azim)


def call(kernel, outs, specs, scratch=(), flops=0):
    shapes = tuple(jax.ShapeDtypeStruct(s, d) for s, d in outs)
    return pl.pallas_call(
        kernel,
        out_shape=shapes,
        in_specs=specs,
        out_specs=(VMEM,) * len(outs),
        scratch_shapes=list(scratch),
        compiler_params=PARAMS,
        cost_estimate=pl.CostEstimate(flops=flops, bytes_accessed=2**20, transcendentals=0),
    )


def pair_swap(value, axes, count, first):
    pairs = []
    for i in range(first, count - 1, 2):
        pairs += [(i, i + 1), (i + 1, i)]
    return lax.ppermute(value, axes, pairs)


def halo_pairs(sizes, partner, spare):
    _, n_ta, n_pa = sizes
    number = lambda place: (place[0] * n_ta + place[1]) * n_pa + place[2]
    inside = lambda place: all(0 <= x < n for x, n in zip(place, sizes))
    pairs = []
    for place in np.ndindex(*sizes):
        other = partner(*place)
        if not inside(other):
            other = spare(*place)
        if inside(other):
            pairs.append((number(place), number(other)))
    return pairs


def radial_partner(row, ta, pa):
    return (row + 1, ta, 0) if pa == 1 else (row - 1, ta, 1)


def polar_partner(first):
    return lambda row, ta, pa: (row, ta + 1 if ta % 2 == first else ta - 1, pa)


def shards(sizes, density, kappa):
    n_row, n_ta, n_pa = sizes
    rows, polar, azim = density.shape
    owners = n_row * n_ta * n_pa
    per = DEGREES // owners
    polar_total, azim_total = polar * n_ta, azim * n_pa
    half = rows // n_pa
    cells = half * polar
    swap = functools.partial(pair_swap, axes="pa", count=n_pa, first=0)

    far, far_kappa = swap(density), swap(kappa)
    (density,) = call(stage_kernel, ((density.shape, F32),), [VMEM])(density)
    (kappa,) = call(stage_kernel, ((kappa.shape, F32),), [VMEM])(kappa)
    ends = ((half, azim_total), F32)
    shell, even, odd = call(
        pack_kernel, (((polar, azim_total), F32), ends, ends), [VMEM] * 2
    )(density, far)
    sides = lambda row, ta, pa: (row, ta ^ 1, pa)
    cores = lambda row, ta, pa: (row, ta, pa ^ 1)
    shell = lax.ppermute(shell, AXES, halo_pairs(sizes, radial_partner, sides))
    even = lax.ppermute(even, AXES, halo_pairs(sizes, polar_partner(0), cores))
    odd = lax.ppermute(odd, AXES, halo_pairs(sizes, polar_partner(1), cores))

    small = small_table(polar_total, azim_total)
    high, low, extra = call(
        functools.partial(table_kernel, sizes),
        (((per * DEGREES, polar_total), BF16),) * 2 + (((2, polar_total), F32),),
        [VMEM] * 2,
        [pltpu.VMEM((per, 2 * DEGREES + 8, 128), F32), pltpu.VMEM((per, DEGREES, polar_total // 2), F32)],
        flops=10**7,
    )(recursion_table(), small)

    waves = wave_table(azim_total, owners)
    (base,) = call(
        functools.partial(early_kernel, sizes), (((cells, azim_total), F32),), [VMEM] * 6
    )(density, far, kappa, far_kappa, *waves)
    keep, send, spec = call(
        functools.partial(stencil_kernel, sizes),
        (((half, polar, azim), F32), ((half, polar, azim), F32), ((2 * DEGREES, cells), F32)),
        [VMEM] * 8,
        [pltpu.VMEM((cells, azim_total), F32)],
    )(base, kappa, far_kappa, shell, even, odd, *waves)

    back = swap(send)
    spread = functools.partial(
        lax.all_to_all, axis_name=AXES, split_axis=0, concat_axis=0, tiled=True
    )
    spec = spread(spec.reshape(owners, 2 * per, cells))

    (spec,) = call(
        functools.partial(solve_kernel, sizes, rows, polar),
        ((spec.shape, F32),),
        [VMEM] * 4,
        [pltpu.VMEM((rows * n_row * 2 * per, polar_total), F32)],
    )(spec, high, low, extra)
    spec = spread(spec).reshape(2 * DEGREES, cells)
    far = swap(spec)
    (updated,) = call(join_kernel, ((density.shape, F32),), [VMEM] * 2)(keep, back)
    (potential,) = call(potential_kernel, ((density.shape, F32),), [VMEM] * 4)(spec, far, *waves)
    return (updated, potential)


def solution(mesh):
    sizes = tuple(mesh.shape[a] for a in AXES)
    placed = (P(*AXES), P(*AXES))

    def body(density, kappa):
        return shards(sizes, density, kappa)

    return jax.shard_map(body, mesh=mesh, in_specs=placed, out_specs=placed, check_vma=False)
```

```python
import functools
import math

import jax
import jax.numpy as jnp
import numpy as np
from jax import lax
from jax.experimental import pallas as pl
from jax.experimental.pallas import tpu as pltpu
from jax.sharding import PartitionSpec as P


DEGREES = 128
AXES = ("row", "ta", "pa")
VMEM = pl.BlockSpec(memory_space=pltpu.VMEM)
ANY = pl.BlockSpec(memory_space=pl.ANY)
PARAMS = pltpu.CompilerParams(vmem_limit_bytes=16 * 2**20)
F32 = jnp.float32
BF16 = jnp.bfloat16
NT = (((1,), (1,)), ((), ()))
NN = (((1,), (0,)), ((), ()))
TN = (((0,), (0,)), ((), ()))


def split(x):
    high = x.astype(BF16)
    return high, (x - high.astype(F32)).astype(BF16)


def dot3(a, b, dims):
    one = functools.partial(lax.dot_general, dimension_numbers=dims, preferred_element_type=F32)
    axis = 1 - dims[0][0][0]
    rows = a[0].shape[axis]
    wide = one(jnp.concatenate(a, axis=axis), b[0])
    return wide[:rows] + (wide[rows:] + one(a[0], b[1]))


def wave_table(azim_total, owners):
    modes = np.arange(DEGREES).reshape(owners, 1, -1, 1)
    phi = (np.arange(azim_total) + 0.5) * (2.0 * math.pi / azim_total)
    both = np.concatenate([np.cos(modes * phi), np.sin(modes * phi)], axis=1)
    table = both.reshape(2 * DEGREES, azim_total)
    high = table.astype(BF16)
    low = (table - high.astype(np.float64)).astype(BF16)
    return jnp.asarray(high), jnp.asarray(low)


def recursion_table():
    l = np.arange(DEGREES, dtype=np.float64)[:, None]
    m = np.arange(DEGREES, dtype=np.float64)[None, :]
    below = m < l
    a = np.sqrt((4 * l * l - 1) / np.where(below, l * l - m * m, 1.0) * below)
    low = l - 1
    b = np.sqrt(np.maximum(low * low - m * m, 0) / np.maximum(4 * low * low - 1, 1.0))
    sect = np.where(l == 1, math.sqrt(3.0), np.sqrt((2 * l + 1) / np.maximum(2 * l, 1.0)))
    wide = np.broadcast_to(sect, (DEGREES, 128))
    spare = np.zeros((8, 128))
    return jnp.asarray(np.concatenate([a, a * b, wide, spare]).astype(np.float32))


def small_table(polar_total, azim_total):
    edge = np.arange(polar_total + 1) * (math.pi / polar_total)
    theta = (np.arange(polar_total) + 0.5) * (math.pi / polar_total)
    band = (np.cos(edge[:-1]) - np.cos(edge[1:])) * (2.0 * math.pi / azim_total)
    x = np.cos(theta)
    mean = np.zeros(polar_total)
    prev, older = np.ones_like(x), np.zeros_like(x)
    for l in range(DEGREES):
        mean[l] = azim_total * np.sum(band * prev)
        n = l + 1
        a = math.sqrt((4 * n * n - 1) / (n * n))
        b = math.sqrt(l * l / max(4 * l * l - 1, 1))
        prev, older = a * (x * prev - b * older), prev
    return jnp.asarray(np.stack([x, np.sin(theta), band, mean]).astype(np.float32))


def owner_of(sizes):
    row, ta, pa = (lax.axis_index(a) for a in AXES)
    return (row * sizes[1] + ta) * sizes[2] + pa


def stage_kernel(source, target):
    target[...] = source[...]


def pack_kernel(rho, far, shell_out, even_out, odd_out):
    rows, polar, azim = rho.shape
    half = rows // 2
    ta, pa = lax.axis_index("ta"), lax.axis_index("pa")
    edge = pa * (rows - 1)
    even = ta % 2 == 0
    for k, part in enumerate((rho, far)):
        at = pl.ds(k * azim, azim)
        shell_out[:, at] = part[edge]
        for r in range(half):
            i = pa * half + r
            first, last = part[i, 0:1, :], part[i, polar - 1 : polar, :]
            even_out[r : r + 1, at] = jnp.where(even, last, first)
            odd_out[r : r + 1, at] = jnp.where(even, first, last)


def both(a, b):
    return jnp.concatenate([a, b], axis=1)


def early_kernel(sizes, rho, far, kappa, far_kappa, w_high, w_low, base):
    rows, polar, azim = rho.shape
    half = rows // 2
    row, ta, pa = (lax.axis_index(a) for a in AXES)
    sub = lax.broadcasted_iota(jnp.int32, (polar, 2 * azim), 0)
    at = lambda i: both(rho[i], far[i])
    turned = lambda x: both(x[:, azim:], x[:, :azim])
    for r in range(half):
        i = pa * half + r
        c = at(i)
        if r == 0:
            edge = jnp.where(row == 0, c, 0.0)
            down = jnp.where(pa == 0, edge, at(jnp.maximum(i - 1, 0)))
        else:
            down = at(i - 1)
        if r == half - 1:
            edge = jnp.where(row == sizes[0] - 1, c, 0.0)
            up = jnp.where(pa == 0, at(jnp.minimum(i + 1, rows - 1)), edge)
        else:
            up = at(i + 1)
        north = jnp.where(ta == 0, turned(c[0:1, :]), 0.0)
        south = jnp.where(ta == sizes[1] - 1, turned(c[polar - 1 :, :]), 0.0)
        pol_up = jnp.where(sub == 0, north, pltpu.roll(c, 1, 0))
        pol_down = jnp.where(sub == polar - 1, south, pltpu.roll(c, polar - 1, 0))
        west = pltpu.roll(c, 1, 1)
        east = pltpu.roll(c, 2 * azim - 1, 1)
        lap = up + down + pol_up + pol_down + west + east - 6.0 * c
        base[r * polar : (r + 1) * polar, :] = c + both(kappa[i], far_kappa[i]) * lap


def stencil_kernel(
    sizes, base, kappa, far_kappa, shell, even_in, odd_in, w_high, w_low, keep, send, spec, cells
):
    rows, polar, azim = kappa.shape
    half = rows // 2
    row, ta, pa = (lax.axis_index(a) for a in AXES)
    even = ta % 2 == 0
    outer = both(shell[:, azim:], shell[:, :azim])
    for r in range(half):
        i = pa * half + r
        k = both(kappa[i], far_kappa[i])
        new = base[r * polar : (r + 1) * polar, :]
        if r == 0:
            new = new + jnp.where((pa == 0) & (row > 0), k * outer, 0.0)
        if r == half - 1:
            new = new + jnp.where((pa == 1) & (row < sizes[0] - 1), k * outer, 0.0)
        one, two = even_in[r : r + 1, :], odd_in[r : r + 1, :]
        north = jnp.where(ta == 0, 0.0, jnp.where(even, two, one)) * k[0:1, :]
        south = jnp.where(ta == sizes[1] - 1, 0.0, jnp.where(even, one, two)) * k[polar - 1 :, :]
        top, low = new[0:8, :], new[polar - 8 :, :]
        sub = lax.broadcasted_iota(jnp.int32, top.shape, 0)
        top = top + jnp.where(sub == 0, north, 0.0)
        low = low + jnp.where(sub == 7, south, 0.0)
        new = jnp.concatenate([top, new[8 : polar - 8, :], low], axis=0)
        keep[r] = new[:, :azim]
        side = half * polar
        for k in range(azim // side):
            spot = pl.ds(k * side + r * polar, polar)
            send[spot, :] = new[:, azim + k * side : azim + (k + 1) * side]
        cells[r * polar : (r + 1) * polar, :] = new - 1.0
    total = None
    for k, place in enumerate((pa, 1 - pa)):
        at = pl.ds(pl.multiple_of(place * azim, azim), azim)
        term = dot3((w_high[:, at], w_low[:, at]), split(cells[:, k * azim : (k + 1) * azim]), NT)
        total = term if total is None else total + term
    spec[...] = total


def table_kernel(sizes, coef_ref, trig_ref, high_ref, low_ref, extra_ref, spread_ref, work):
    per, degrees, north = work.shape
    extra_ref[...] = trig_ref[2:4, :]
    start = owner_of(sizes) * per
    lanes = 128
    near = pltpu.roll(coef_ref[: 2 * degrees, :], lanes - start, 1)
    for q in range(per):
        spread_ref[q, : 2 * degrees, :] = jnp.broadcast_to(near[:, q : q + 1], (2 * degrees, lanes))
    parts = north // lanes
    cut = lambda row, k: jnp.broadcast_to(trig_ref[row : row + 1, k * lanes : (k + 1) * lanes], (8, lanes))
    cos_t = [cut(0, k) for k in range(parts)]
    sin_t = [cut(1, k) for k in range(parts)]
    sub = lax.broadcasted_iota(jnp.int32, (8, lanes), 0)

    def block(step, carry):
        sect, prev, older = carry
        base = pl.multiple_of(step * 8, 8)
        tiles = [[jnp.zeros((8, lanes), F32)] * parts for _ in range(per)]
        for inner in range(8):
            l = base + inner
            factor = coef_ref[pl.ds(2 * degrees + l, 8, stride=0), :]
            grown = [s * (factor * sin_t[k]) for k, s in enumerate(sect)]
            if inner == 0:
                grown = [jnp.where(step == 0, s, g) for s, g in zip(sect, grown)]
            sect = grown
            fresh = []
            for q in range(per):
                a = spread_ref[q, pl.ds(l, 8, stride=0), :]
                ab = spread_ref[q, pl.ds(degrees + l, 8, stride=0), :]
                seed = l == start + q
                line = []
                for k in range(parts):
                    rest = jnp.where(seed, sect[k], 0.0) - ab * older[q][k]
                    new = (a * cos_t[k]) * prev[q][k] + rest
                    tiles[q][k] = jnp.where(sub == inner, new, tiles[q][k])
                    line.append(new)
                fresh.append(line)
            prev, older = fresh, prev
        for q in range(per):
            for k in range(parts):
                work[q, pl.ds(base, 8), k * lanes : (k + 1) * lanes] = tiles[q][k]
        return sect, prev, older

    zero = [[jnp.zeros((8, lanes), F32)] * parts for _ in range(per)]
    lax.fori_loop(0, degrees // 8, block, ([jnp.ones((8, lanes), F32)] * parts, zero, zero))
    square = lambda d: lax.broadcasted_iota(jnp.int32, (north, north), d)
    mirror = jnp.where(square(0) + square(1) == north - 1, 1.0, 0.0).astype(BF16)
    row = lax.broadcasted_iota(jnp.int32, (8, north), 0)
    for q in range(per):
        even = ((row + (start + q)) & 1) == 0
        sign = jnp.concatenate([jnp.where(even, 1.0, -1.0)] * (degrees // 8), axis=0)
        at = pl.ds(q * degrees, degrees)
        for piece, ref in zip(split(work[q]), (high_ref, low_ref)):
            ref[at, :north] = piece
            flipped = lax.dot_general(piece, mirror, NN, preferred_element_type=F32)
            ref[at, north:] = (sign * flipped).astype(BF16)


def solve_kernel(sizes, rows, polar, spec_ref, high_ref, low_ref, extra_ref, out_ref, work_ref):
    n_row, n_ta, n_pa = sizes
    shells = rows * n_row
    pair = spec_ref.shape[1]
    per = pair // 2
    degrees = high_ref.shape[0] // per
    half = rows // n_pa
    band = extra_ref[0:1, :]
    for g in range(n_row):
        for h in range(n_pa):
            parts = [spec_ref[(g * n_ta + t) * n_pa + h] for t in range(n_ta)]
            for r in range(half):
                piece = jnp.concatenate([x[:, r * polar : (r + 1) * polar] for x in parts], axis=1)
                work_ref[pl.ds((g * rows + h * half + r) * pair, pair), :] = piece * band
    table = high_ref[...], low_ref[...]
    wide = dot3(split(work_ref[...]), table, NT)
    slot = lax.broadcasted_iota(jnp.int32, (shells * pair, degrees), 0) & (per - 1)
    picked = wide[:, :degrees]
    for q in range(1, per):
        picked = jnp.where(slot == q, wide[:, q * degrees : (q + 1) * degrees], picked)
    log_eight = math.log(8.0)
    step = log_eight / shells
    degree = lax.broadcasted_iota(jnp.int32, (pair, degrees), 1).astype(F32)
    decay_in = jnp.exp(-step * degree)
    decay_out = jnp.exp(-step * (degree + 1.0))
    scale = jnp.where(degree > 0.0, -1.0 / (4.0 * math.pi * (2.0 * degree + 1.0)), 0.0)
    edges = np.exp(log_eight * (np.arange(shells + 1) / shells - 1.0))
    volume = (edges[1:] ** 3 - edges[:-1] ** 3) / 3.0
    radii = np.exp(log_eight * ((np.arange(shells) + 0.5) / shells - 1.0))
    sub = lax.broadcasted_iota(jnp.int32, (pair, degrees), 0)
    mean = jnp.where((sub == 0) & (owner_of(sizes) == 0), extra_ref[1:2, :degrees], 0.0)
    picked = [picked[i * pair : (i + 1) * pair] + mean for i in range(shells)]
    moments = [picked[i] * float(volume[i]) for i in range(shells)]
    sums = []
    carry = jnp.zeros((pair, degrees), F32)
    for i in range(shells):
        carry = carry * decay_in + moments[i]
        sums.append(carry)
    carry = jnp.zeros((pair, degrees), F32)
    for i in reversed(range(shells)):
        sums[i] = (sums[i] + carry) * (scale * float(1.0 / radii[i]))
        carry = (carry + moments[i]) * decay_out
    coeffs = jnp.concatenate(sums, axis=0)
    spread = jnp.concatenate([jnp.where(slot == q, coeffs, 0.0) for q in range(per)], axis=1)
    field = dot3(split(spread), table, NN)
    for g in range(n_row):
        for h in range(n_pa):
            for t in range(n_ta):
                pieces = []
                for r in range(half):
                    i = g * rows + h * half + r
                    pieces.append(field[i * pair : (i + 1) * pair, t * polar : (t + 1) * polar])
                out_ref[(g * n_ta + t) * n_pa + h] = jnp.concatenate(pieces, axis=1)


def half_field(spec, w_high, w_low, place):
    azim = w_high.shape[1] // 2
    at = pl.ds(pl.multiple_of(place * azim, azim), azim)
    return dot3(split(spec), (w_high[:, at], w_low[:, at]), TN)


def near_kernel(spec, w_high, w_low, pot, work, sem):
    half = work.shape[0]
    pa = lax.axis_index("pa")
    work[...] = half_field(spec[...], w_high, w_low, pa).reshape(work.shape)
    copy = pltpu.make_async_copy(work, pot.at[pl.ds(pa * half, half)], sem)
    copy.start()
    copy.wait()


def merge_kernel(spec, send, out):
    size = spec.shape[0]
    out[:size, :] = spec[...]
    out[size:, :] = send[...]


def far_kernel(keep, both, w_high, w_low, _, upd, pot, back, work, sems):
    half, polar, azim = work.shape
    size = w_high.shape[0]
    side = half * polar
    pa = lax.axis_index("pa")
    mine, other = pl.ds(pa * half, half), pl.ds((1 - pa) * half, half)
    copies = [
        pltpu.make_async_copy(keep, upd.at[mine], sems.at[0]),
        pltpu.make_async_copy(back, upd.at[other], sems.at[1]),
        pltpu.make_async_copy(work, pot.at[other], sems.at[2]),
    ]
    copies[0].start()
    for k in range(azim // side):
        piece = both[size + k * side : size + (k + 1) * side, :]
        back[:, :, k * side : (k + 1) * side] = piece.reshape(half, polar, side)
    copies[1].start()
    work[...] = half_field(both[:size, :], w_high, w_low, pa).reshape(work.shape)
    copies[2].start()
    for copy in copies:
        copy.wait()


def call(kernel, outs, specs, scratch=(), flops=0, place=VMEM, aliases={}):
    shapes = tuple(jax.ShapeDtypeStruct(s, d) for s, d in outs)
    return pl.pallas_call(
        kernel,
        out_shape=shapes,
        in_specs=specs,
        out_specs=(place,) * len(outs),
        input_output_aliases=aliases,
        scratch_shapes=list(scratch),
        compiler_params=PARAMS,
        cost_estimate=pl.CostEstimate(flops=flops, bytes_accessed=2**20, transcendentals=0),
    )


def pair_swap(value, axes, count, first):
    pairs = []
    for i in range(first, count - 1, 2):
        pairs += [(i, i + 1), (i + 1, i)]
    return lax.ppermute(value, axes, pairs)


def halo_pairs(sizes, partner, spare):
    _, n_ta, n_pa = sizes
    number = lambda place: (place[0] * n_ta + place[1]) * n_pa + place[2]
    inside = lambda place: all(0 <= x < n for x, n in zip(place, sizes))
    pairs = []
    for place in np.ndindex(*sizes):
        other = partner(*place)
        if not inside(other):
            other = spare(*place)
        if inside(other):
            pairs.append((number(place), number(other)))
    return pairs


def radial_partner(row, ta, pa):
    return (row + 1, ta, 0) if pa == 1 else (row - 1, ta, 1)


def polar_partner(first):
    return lambda row, ta, pa: (row, ta + 1 if ta % 2 == first else ta - 1, pa)


def shards(sizes, density, kappa):
    n_row, n_ta, n_pa = sizes
    rows, polar, azim = density.shape
    owners = n_row * n_ta * n_pa
    per = DEGREES // owners
    polar_total, azim_total = polar * n_ta, azim * n_pa
    half = rows // n_pa
    cells = half * polar
    swap = functools.partial(pair_swap, axes="pa", count=n_pa, first=0)

    far, far_kappa = swap(density), swap(kappa)
    (density,) = call(stage_kernel, ((density.shape, F32),), [VMEM])(density)
    (kappa,) = call(stage_kernel, ((kappa.shape, F32),), [VMEM])(kappa)
    ends = ((half, azim_total), F32)
    shell, even, odd = call(
        pack_kernel, (((polar, azim_total), F32), ends, ends), [VMEM] * 2
    )(density, far)
    sides = lambda row, ta, pa: (row, ta ^ 1, pa)
    cores = lambda row, ta, pa: (row, ta, pa ^ 1)
    shell = lax.ppermute(shell, AXES, halo_pairs(sizes, radial_partner, sides))
    even = lax.ppermute(even, AXES, halo_pairs(sizes, polar_partner(0), cores))
    odd = lax.ppermute(odd, AXES, halo_pairs(sizes, polar_partner(1), cores))

    small = small_table(polar_total, azim_total)
    high, low, extra = call(
        functools.partial(table_kernel, sizes),
        (((per * DEGREES, polar_total), BF16),) * 2 + (((2, polar_total), F32),),
        [VMEM] * 2,
        [pltpu.VMEM((per, 2 * DEGREES + 8, 128), F32), pltpu.VMEM((per, DEGREES, polar_total // 2), F32)],
        flops=10**7,
    )(recursion_table(), small)

    waves = wave_table(azim_total, owners)
    (base,) = call(
        functools.partial(early_kernel, sizes), (((cells, azim_total), F32),), [VMEM] * 6
    )(density, far, kappa, far_kappa, *waves)
    keep, send, spec = call(
        functools.partial(stencil_kernel, sizes),
        (((half, polar, azim), F32), ((azim, cells), F32), ((2 * DEGREES, cells), F32)),
        [VMEM] * 8,
        [pltpu.VMEM((cells, azim_total), F32)],
    )(base, kappa, far_kappa, shell, even, odd, *waves)

    spread = functools.partial(
        lax.all_to_all, axis_name=AXES, split_axis=0, concat_axis=0, tiled=True
    )
    spec = spread(spec.reshape(owners, 2 * per, cells))

    (spec,) = call(
        functools.partial(solve_kernel, sizes, rows, polar),
        ((spec.shape, F32),),
        [VMEM] * 4,
        [pltpu.VMEM((rows * n_row * 2 * per, polar_total), F32)],
    )(spec, high, low, extra)
    spec = spread(spec).reshape(2 * DEGREES, cells)
    (both,) = call(merge_kernel, (((2 * DEGREES + azim, cells), F32),), [VMEM] * 2)(spec, send)
    far = swap(both)
    whole = (density.shape, F32)
    work = pltpu.VMEM((half, polar, azim), F32)
    (potential,) = call(
        near_kernel, (whole,), [VMEM] * 3, [work, pltpu.SemaphoreType.DMA], place=ANY
    )(spec, *waves)
    updated, potential = call(
        far_kernel, (whole, whole), [VMEM] * 4 + [ANY],
        [work, work, pltpu.SemaphoreType.DMA((3,))], place=ANY, aliases={4: 1},
    )(keep, far, *waves, potential)
    return (updated, potential)


def solution(mesh):
    sizes = tuple(mesh.shape[a] for a in AXES)
    placed = (P(*AXES), P(*AXES))

    def body(density, kappa):
        return shards(sizes, density, kappa)

    return jax.shard_map(body, mesh=mesh, in_specs=placed, out_specs=placed, check_vma=False)
```
